128 devices in a mesh: seq: 64 (over z_lo, x, y, core), trace: 2 (over z_hi).
Axes of the slice: x: 4, y: 4, z: 4 (z_hi: 2, z_lo: 2; z = z_hi * 2 + z_lo), core: 2. Of those that a mesh axis runs over, the one named last changes fastest.
Arguments:
- signal: bfloat16 [4, 32768, 256], P('trace', 'seq'), may hold values from -6 to 6
- cotangent: bfloat16 [4, 32768, 256], P('trace', 'seq'), may hold values from -6 to 6
- filter_taps: bfloat16 [32768, 256], P('seq'), may hold values from -6 to 6
Outputs:
- input_grad: float32 [4, 32768, 256], P('trace', 'seq')
- filter_grad: float32 [32768, 256], P('seq')
The draws below stay inside these ranges and needn't reach their ends.
All inputs are finite; a program needn't handle non-finite values.
Results may differ from the reference program's by a relative error of at most 0.0003.
Values may be sent and summed in bfloat16 or wider, within the bound.
A program may use at most 128 MiB of HBM per device.

```python
import jax
import jax.numpy as jnp

CHANNELS = 256
LENGTH = 32768
TRACES = 4


def steps_of(own_key, dims, pieces, least, largest):
    level, own = 1.0, jax.random.fold_in(own_key, 6)
    for position, parts in pieces:
        draws = jnp.exp(jax.random.uniform(jax.random.fold_in(own, position), (parts,), jnp.float32, least / len(pieces), largest / len(pieces)))
        level = level * jnp.repeat(draws, dims[position] // parts).reshape([-1 if axis == position else 1 for axis in range(len(dims))])
    return level


def centred(own_key, dims, width, bound, shards=(), held_as=jnp.bfloat16):
    level = steps_of(own_key, dims, shards, -0.22, 0.18) if shards else 1.0
    array = jax.random.normal(own_key, dims, jnp.float32) * width * level
    return jnp.minimum(jnp.maximum(array, -bound), bound).astype(held_as)


def setup_inputs(seed: int = 0) -> dict:
    seeds = jax.random.split(jax.random.key(seed), 4)
    return {
        "signal": centred(seeds[0], (TRACES, LENGTH, CHANNELS), 1.0, 6.0, ((0, 2), (1, 64))),
        "cotangent": centred(seeds[1], (TRACES, LENGTH, CHANNELS), 1.0, 6.0, ((0, 2), (1, 64))),
        "filter_taps": centred(seeds[2], (LENGTH, CHANNELS), 1.0, 6.0, ((0, 64),)),
    }


def reference(signal, cotangent, filter_taps):
    padded = 2 * LENGTH
    factor = 1.0 / (LENGTH ** 0.5)
    taps_spec = jnp.fft.rfft(filter_taps.astype(jnp.float32), n=padded, axis=0)
    input_grads = []
    grad_spec = None
    for trace_id in range(TRACES):
        signal_spec = jnp.fft.rfft(signal[trace_id].astype(jnp.float32), n=padded, axis=0)
        upstream = jnp.fft.rfft(cotangent[trace_id].astype(jnp.float32), n=padded, axis=0)
        backward = jnp.fft.irfft(jnp.conj(taps_spec) * upstream, n=padded, axis=0)[:LENGTH]
        input_grads.append((backward * factor).astype(jnp.float32))
        product = jnp.conj(signal_spec) * upstream
        grad_spec = product if grad_spec is None else grad_spec + product
    filter_grad = jnp.fft.irfft(grad_spec, n=padded, axis=0)[:LENGTH] * factor
    return jnp.stack(input_grads, axis=0), filter_grad.astype(jnp.float32)
```

```python
import math

import jax
import jax.numpy as jnp
import numpy as np
from jax import lax
from jax.experimental import pallas as pl
from jax.experimental.pallas import tpu as pltpu
from jax.sharding import PartitionSpec as P

LANES = 128
STRIDE = 37
MESH = pl.DeviceIdType.MESH
F32 = jnp.float32
BF16 = jnp.bfloat16


def halves(values):
    high = np.asarray(values, np.float32).astype(jnp.bfloat16)
    low = (values - high.astype(np.float64)).astype(jnp.bfloat16)
    return high, low


def tables(seq_count, pieces):
    rows = seq_count * pieces
    length = rows * LANES
    order = (np.arange(seq_count)[None, :] * pieces + np.arange(pieces)[:, None]).reshape(-1)
    odd = np.arange(rows) + 0.5
    angle = 2.0 * math.pi * odd[:, None] * order[None, :] / (2 * rows)
    split = np.concatenate([np.cos(angle), -np.sin(angle)], axis=0)
    scale = (2.0 / (2 * length)) / math.sqrt(length)
    join = np.concatenate([np.cos(angle.T), -np.sin(angle.T)], axis=1) * scale
    turn = 2.0 * math.pi * odd[:, None] * np.arange(LANES)[None, :] / (2 * length)
    inner = 2.0 * math.pi * np.outer(np.arange(LANES), np.arange(LANES)) / LANES
    cos, sin = np.cos(inner), np.sin(inner)
    ahead = np.block([[cos, -sin], [sin, cos]])
    back = np.block([[cos, sin], [-sin, cos]])
    turns = np.stack([np.cos(turn), -np.sin(turn)]).astype(np.float32)
    stack = lambda values: np.stack(halves(values))
    return stack(split), stack(join), stack(ahead), stack(back), turns


def parts_of(values):
    high = values.astype(BF16)
    return high, (values - high.astype(F32)).astype(BF16)


def dot(left, right):
    return jnp.dot(left, right, preferred_element_type=F32)


def kernel(seq_count, trace_groups, cot, taps, sig, split_h, join_h, ahead_h, back_h, turns_h,
           input_out, filter_out, split, join, ahead, back, turns, send_c, send_t, send_s,
           recv_c, recv_t, recv_s, sequences, spectra, out_i, out_f, in_i, in_f,
           const_sem, send_sem, recv_sem):
    total = seq_count * trace_groups
    held, span, channels = cot.shape
    own = channels // total
    pieces = span // LANES
    traces = held * trace_groups
    rows = seq_count * pieces
    seq = lax.axis_index("seq")
    group = lax.axis_index("trace")
    me = group * seq_count + seq
    barrier = pltpu.get_barrier_semaphore()

    consts = [
        pltpu.make_async_copy(src, dst, const_sem.at[n])
        for n, (src, dst) in enumerate(
            [(split_h, split), (join_h, join), (ahead_h, ahead), (back_h, back), (turns_h, turns)]
        )
    ]
    for copy in consts:
        copy.start()

    def place(target):
        return (lax.rem(target, seq_count), lax.div(target, seq_count))

    def other(step):
        return lax.rem(me + step * STRIDE, total)

    def greet(step, carry):
        pl.semaphore_signal(barrier, inc=1, device_id=place(other(step)), device_id_type=MESH)
        return carry

    lax.fori_loop(1, total, greet, 0)

    def spread(block):
        turned = block.T
        return [
            turned[c * total : (c + 1) * total, m * LANES : (m + 1) * LANES]
            for c in range(own)
            for m in range(pieces)
        ]

    def stage(items, target):
        listed = [piece for item in items for piece in spread(item)]
        target[...] = jnp.swapaxes(jnp.stack(listed), 0, 1)

    stage([taps[...]], send_t)
    stage([cot[i] for i in range(held)], send_c)
    stage([sig[i] for i in range(held)], send_s)
    recv_t[seq] = send_t[me]
    recv_c[me] = send_c[me]
    recv_s[me] = send_s[me]
    pl.semaphore_wait(barrier, total - 1)

    def push(source, target, slot, device):
        pltpu.make_async_remote_copy(
            src_ref=source,
            dst_ref=target,
            send_sem=send_sem.at[slot],
            recv_sem=recv_sem.at[slot],
            device_id=place(device),
            device_id_type=MESH,
        ).start()

    def send_taps(step, carry):
        target = group * seq_count + lax.rem(seq + step * STRIDE, seq_count)
        push(send_t.at[target], recv_t.at[seq], 0, target)
        return carry

    def send_cot(step, carry):
        push(send_c.at[other(step)], recv_c.at[me], 1, other(step))
        return carry

    def send_sig(step, carry):
        push(send_s.at[other(step)], recv_s.at[me], 2, other(step))
        return carry

    lax.fori_loop(1, seq_count, send_taps, 0)
    lax.fori_loop(1, total, send_cot, 0)
    lax.fori_loop(1, total, send_sig, 0)

    def arrive(ref, count, slot):
        view = ref.at[pl.ds(0, count)]
        pltpu.make_async_copy(view, view, recv_sem.at[slot]).wait()

    def depart(ref, count, slot):
        view = ref.at[pl.ds(0, count)]
        pltpu.make_async_copy(view, view, send_sem.at[slot]).wait()

    for copy in consts:
        copy.wait()

    def gather(block, count, first):
        moved = jnp.swapaxes(block, 0, 1)
        for i in range(count):
            columns = []
            for c in range(own):
                start = (i * own + c) * pieces
                columns.append(jnp.concatenate([moved[start + m] for m in range(pieces)], axis=0))
            sequences[first + i] = jnp.concatenate(columns, axis=1)

    def ahead_item(n, carry):
        values = sequences[n]
        first = dot(split[0], values) + dot(split[1], values)
        real, imag = first[:rows], first[rows:]
        for c in range(own):
            lanes = slice(c * LANES, (c + 1) * LANES)
            re, im = real[:, lanes], imag[:, lanes]
            turned = jnp.concatenate(
                [re * turns[0] - im * turns[1], re * turns[1] + im * turns[0]], axis=1
            )
            high, low = parts_of(turned)
            spectra[n, c] = dot(high, ahead[0]) + dot(low, ahead[0]) + dot(high, ahead[1])
        return carry

    def back_item(products):
        highs, lows = [], []
        for product in products:
            high, low = parts_of(product)
            mid = dot(high, back[0]) + dot(low, back[0]) + dot(high, back[1])
            re, im = mid[:, :LANES], mid[:, LANES:]
            turned = jnp.concatenate(
                [re * turns[0] + im * turns[1], im * turns[0] - re * turns[1]], axis=0
            )
            high, low = parts_of(turned)
            highs.append(high)
            lows.append(low)
        high = jnp.concatenate(highs, axis=1)
        low = jnp.concatenate(lows, axis=1)
        return dot(join[0], high) + dot(join[0], low) + dot(join[1], high)

    def turned_product(left, right):
        lr, li = left[:, :LANES], left[:, LANES:]
        rr, ri = right[:, :LANES], right[:, LANES:]
        return jnp.concatenate([lr * rr + li * ri, lr * ri - li * rr], axis=1)

    def cut(values):
        return [
            values[m * seq_count : (m + 1) * seq_count, c * LANES : (c + 1) * LANES]
            for c in range(own)
            for m in range(pieces)
        ]

    arrive(recv_t, seq_count - 1, 0)
    gather(recv_t[...], 1, 0)
    arrive(recv_c, total - 1, 1)
    for other_group in range(trace_groups):
        gather(recv_c[other_group * seq_count : (other_group + 1) * seq_count], held,
               1 + other_group * held)
    lax.fori_loop(0, 1 + traces, ahead_item, 0)

    def input_group(other_group, carry):
        listed = []
        for i in range(held):
            n = 1 + other_group * held + i
            listed += cut(back_item([turned_product(spectra[0, c], spectra[n, c]) for c in range(own)]))
        base = pl.multiple_of(other_group * seq_count, seq_count)
        out_i[pl.ds(base, seq_count)] = jnp.swapaxes(jnp.stack(listed), 0, 1)
        return carry

    lax.fori_loop(0, trace_groups, input_group, 0)
    in_i[me] = out_i[me]

    def send_input(step, carry):
        push(out_i.at[other(step)], in_i.at[me], 3, other(step))
        return carry

    lax.fori_loop(1, total, send_input, 0)

    arrive(recv_s, total - 1, 2)
    for other_group in range(trace_groups):
        gather(recv_s[other_group * seq_count : (other_group + 1) * seq_count], held,
               1 + traces + other_group * held)
    lax.fori_loop(1 + traces, 1 + 2 * traces, ahead_item, 0)
    sums = []
    for c in range(own):
        acc = None
        for b in range(traces):
            product = turned_product(spectra[1 + traces + b, c], spectra[1 + b, c])
            acc = product if acc is None else acc + product
        sums.append(acc)
    out_f[...] = jnp.swapaxes(jnp.stack(cut(back_item(sums))), 0, 1)
    in_f[me] = out_f[seq]

    def send_filter(step, carry):
        push(out_f.at[lax.rem(other(step), seq_count)], in_f.at[me], 4, other(step))
        return carry

    lax.fori_loop(1, total, send_filter, 0)

    def settle(block, i):
        return block[i].T

    arrive(in_i, total - 1, 3)
    moved = jnp.swapaxes(in_i[...], 0, 1)
    for i in range(held):
        for c in range(own):
            for m in range(pieces):
                input_out[i, m * LANES : (m + 1) * LANES, c * total : (c + 1) * total] = moved[
                    (i * own + c) * pieces + m
                ].T
    arrive(in_f, total - 1, 4)
    moved = jnp.swapaxes(in_f[...], 0, 1)
    for c in range(own):
        for m in range(pieces):
            filter_out[m * LANES : (m + 1) * LANES, c * total : (c + 1) * total] = moved[
                c * pieces + m
            ].T
    depart(recv_t, seq_count - 1, 0)
    depart(recv_c, total - 1, 1)
    depart(recv_s, total - 1, 2)
    depart(in_i, total - 1, 3)
    depart(in_f, total - 1, 4)


def local(seq_count, trace_groups, signal, cotangent, filter_taps):
    total = seq_count * trace_groups
    held, span, channels = signal.shape
    own = channels // total
    pieces = span // LANES
    rows = seq_count * pieces
    items = 1 + 2 * held * trace_groups
    constants = [jnp.asarray(table) for table in tables(seq_count, pieces)]
    wide, thin = held * own * pieces, own * pieces
    vmem = pl.BlockSpec(memory_space=pltpu.VMEM)
    anywhere = pl.BlockSpec(memory_space=pl.ANY)

    def body(*refs):
        kernel(seq_count, trace_groups, *refs)

    return pl.pallas_call(
        body,
        out_shape=(
            jax.ShapeDtypeStruct((held, span, channels), F32),
            jax.ShapeDtypeStruct((span, channels), F32),
        ),
        in_specs=[vmem] * 3 + [anywhere] * len(constants),
        out_specs=(vmem, vmem),
        scratch_shapes=[pltpu.VMEM(table.shape, table.dtype) for table in constants]
        + [
            pltpu.VMEM((total, wide, LANES), BF16),
            pltpu.VMEM((total, thin, LANES), BF16),
            pltpu.VMEM((total, wide, LANES), BF16),
            pltpu.VMEM((total, wide, LANES), BF16),
            pltpu.VMEM((seq_count, thin, LANES), BF16),
            pltpu.VMEM((total, wide, LANES), BF16),
            pltpu.VMEM((items, rows, own * LANES), BF16),
            pltpu.VMEM((items, own, rows, 2 * LANES), F32),
            pltpu.VMEM((total, wide, LANES), F32),
            pltpu.VMEM((seq_count, thin, LANES), F32),
            pltpu.VMEM((total, wide, LANES), F32),
            pltpu.VMEM((total, thin, LANES), F32),
            pltpu.SemaphoreType.DMA((len(constants),)),
            pltpu.SemaphoreType.DMA((5,)),
            pltpu.SemaphoreType.DMA((5,)),
        ],
        name="correlate",
        compiler_params=pltpu.CompilerParams(
            collective_id=0, has_side_effects=True, vmem_limit_bytes=56 << 20
        ),
    )(cotangent, filter_taps, signal, *constants)


def solution(mesh):
    seq_count, trace_groups = mesh.shape["seq"], mesh.shape["trace"]

    def run(signal, cotangent, filter_taps):
        return local(seq_count, trace_groups, signal, cotangent, filter_taps)

    in_specs = (P("trace", "seq", None), P("trace", "seq", None), P("seq", None))
    out_specs = (P("trace", "seq", None), P("seq", None))
    return jax.shard_map(run, mesh=mesh, in_specs=in_specs, out_specs=out_specs, check_vma=False)
```

```python
import math

import jax
import jax.numpy as jnp
import numpy as np
from jax import lax
from jax.experimental import pallas as pl
from jax.experimental.pallas import tpu as pltpu
from jax.sharding import PartitionSpec as P

LANES = 128
STRIDE = 37
POWER = 9
CEILING = 2.0**14
MESH = pl.DeviceIdType.MESH
F32 = jnp.float32
BF16 = jnp.bfloat16


def halves(values):
    high = np.asarray(values, np.float32).astype(jnp.bfloat16)
    low = (values - high.astype(np.float64)).astype(jnp.bfloat16)
    return high, low


def tables(seq_count, pieces):
    rows = seq_count * pieces
    length = rows * LANES
    near = np.arange(rows // 2) + 0.5
    odd = np.concatenate([near, rows - near])
    scale = (2.0 / (2 * length)) / math.sqrt(length)
    splits, joins = [], []
    for parity in range(2):
        order = np.concatenate(
            [np.arange(seq_count) * pieces + m for m in range(parity, pieces, 2)]
        )
        angle = 2.0 * math.pi * near[:, None] * order[None, :] / (2 * rows)
        high, low = halves(np.concatenate([np.cos(angle), -np.sin(angle)], axis=0))
        splits.append(np.concatenate([high, low], axis=1))
        joins.append(
            np.stack(halves(np.concatenate([np.cos(angle.T), -np.sin(angle.T)], axis=1) * scale))
        )
    turn = 2.0 * math.pi * odd[:, None] * np.arange(LANES)[None, :] / (2 * length)
    inner = 2.0 * math.pi * np.outer(np.arange(LANES), np.arange(LANES)) / LANES
    cos, sin = np.cos(inner), np.sin(inner)
    ahead = np.block([[cos, -sin], [sin, cos]])
    back = np.block([[cos, sin], [-sin, cos]])
    turns = np.stack([np.cos(turn), -np.sin(turn)]).astype(np.float32)
    return np.stack(splits), np.stack(joins), np.stack(halves(ahead)), np.stack(halves(back)), turns


def parts_of(values):
    high = values.astype(BF16)
    return high, (values - high.astype(F32)).astype(BF16)


def dot(left, right):
    return jnp.dot(left, right, preferred_element_type=F32)


def kernel(seq_count, trace_groups, near_count, cot_h, taps_h, sig_h, split_h, join_h, ahead_h,
           back_h, turns_h, input_out, filter_out, cot, taps, sig, split, join, ahead, back, turns,
           send_c, send_t, send_s, recv_c, recv_t, recv_s, peak, peaks_near, peak_far, peaks_far,
           sequences, spectra, out_i, out_f, in_i, in_f, done_i, done_f,
           load_sem, store_sem, send_sem, recv_sem):
    total = seq_count * trace_groups
    held, span, channels = cot.shape
    own = channels // total
    pieces = span // LANES
    traces = held * trace_groups
    rows = seq_count * pieces
    half = rows // 2
    far_count = total // near_count
    seq = lax.axis_index("seq")
    group = lax.axis_index("trace")
    me = group * seq_count + seq
    barrier = pltpu.get_barrier_semaphore()

    loads = [
        pltpu.make_async_copy(src, dst, load_sem.at[n])
        for n, (src, dst) in enumerate(
            [(cot_h, cot), (taps_h, taps), (sig_h, sig), (split_h, split), (join_h, join),
             (ahead_h, ahead), (back_h, back), (turns_h, turns)]
        )
    ]
    for copy in loads:
        copy.start()

    def place(target):
        return (lax.rem(target, seq_count), lax.div(target, seq_count))

    def other(step):
        return lax.rem(me + step * STRIDE, total)

    def greet(step, carry):
        pl.semaphore_signal(barrier, inc=1, device_id=place(other(step)), device_id_type=MESH)
        return carry

    lax.fori_loop(1, total, greet, 0)

    def spread(block):
        turned = block.T
        return [
            turned[c * total : (c + 1) * total, m * LANES : (m + 1) * LANES]
            for c in range(own)
            for m in range(pieces)
        ]

    def stage(items, target):
        listed = [piece for item in items for piece in spread(item)]
        target[...] = jnp.swapaxes(jnp.stack(listed), 0, 1)

    def largest(values):
        return jnp.max(jnp.abs(values.astype(F32)))

    for copy in loads[:3]:
        copy.wait()
    stage([taps[...]], send_t)
    stage([cot[i] for i in range(held)], send_c)
    stage([sig[i] for i in range(held)], send_s)
    recv_t[seq] = send_t[me]
    recv_c[me] = send_c[me]
    recv_s[me] = send_s[me]
    lane = lax.broadcasted_iota(jnp.int32, (1, LANES), 1)
    peak[...] = jnp.where(
        lane == 0, largest(cot[...]), jnp.where(lane == 1, largest(taps[...]), largest(sig[...]))
    )
    first = lax.div(me, near_count)
    second = lax.rem(me, near_count)
    peaks_near[second] = peak[...]
    pl.semaphore_wait(barrier, total - 1)

    def push(source, target, slot, device):
        pltpu.make_async_remote_copy(
            src_ref=source,
            dst_ref=target,
            send_sem=send_sem.at[slot],
            recv_sem=recv_sem.at[slot],
            device_id=place(device),
            device_id_type=MESH,
        ).start()

    def send_near(step, carry):
        target = first * near_count + lax.rem(second + step, near_count)
        push(peak, peaks_near.at[second], 5, target)
        return carry

    def send_far(step, carry):
        target = lax.rem(first + step, far_count) * near_count + second
        push(peak_far, peaks_far.at[first], 6, target)
        return carry

    def send_taps(step, carry):
        target = group * seq_count + lax.rem(seq + step * STRIDE, seq_count)
        push(send_t.at[target], recv_t.at[seq], 0, target)
        return carry

    def send_cot(step, carry):
        push(send_c.at[other(step)], recv_c.at[me], 1, other(step))
        return carry

    def send_sig(step, carry):
        push(send_s.at[other(step)], recv_s.at[me], 2, other(step))
        return carry

    def arrive(ref, count, slot):
        view = ref.at[pl.ds(0, count)]
        pltpu.make_async_copy(view, view, recv_sem.at[slot]).wait()

    def depart(ref, count, slot):
        view = ref.at[pl.ds(0, count)]
        pltpu.make_async_copy(view, view, send_sem.at[slot]).wait()

    lax.fori_loop(1, near_count, send_near, 0)
    lax.fori_loop(1, seq_count, send_taps, 0)
    lax.fori_loop(1, total, send_cot, 0)
    arrive(peaks_near, near_count - 1, 5)
    peak_far[...] = jnp.max(peaks_near[...], axis=0)
    peaks_far[first] = peak_far[...]
    lax.fori_loop(1, far_count, send_far, 0)
    lax.fori_loop(1, total, send_sig, 0)
    for copy in loads[3:]:
        copy.wait()

    def gather(block, count, start):
        moved = jnp.swapaxes(block, 0, 1)
        for i in range(count):
            for parity in range(2):
                columns = []
                for c in range(own):
                    base = (i * own + c) * pieces
                    columns.append(
                        jnp.concatenate(
                            [moved[base + m] for m in range(parity, pieces, 2)], axis=0
                        )
                    )
                sequences[start + i, parity] = jnp.concatenate(columns, axis=1)

    def ahead_item(n, carry):
        sides = []
        for parity in range(2):
            values = sequences[n, parity]
            sides.append(dot(split[parity], jnp.concatenate([values, values], axis=0)))
        even_re, even_im = sides[0][:half], sides[0][half:]
        odd_re, odd_im = sides[1][:half], sides[1][half:]
        real = jnp.concatenate([even_re + odd_re, even_re - odd_re], axis=0)
        imag = jnp.concatenate([even_im + odd_im, odd_im - even_im], axis=0)
        for c in range(own):
            lanes = slice(c * LANES, (c + 1) * LANES)
            re, im = real[:, lanes], imag[:, lanes]
            turned = jnp.concatenate(
                [re * turns[0] - im * turns[1], re * turns[1] + im * turns[0]], axis=1
            )
            high, low = parts_of(turned)
            spectra[n, c] = dot(high, ahead[0]) + dot(low, ahead[0]) + dot(high, ahead[1])
        return carry

    def back_item(products):
        sides = [[], []]
        for product in products:
            high, low = parts_of(product)
            mid = dot(high, back[0]) + dot(low, back[0]) + dot(high, back[1])
            re, im = mid[:, :LANES], mid[:, LANES:]
            real = re * turns[0] + im * turns[1]
            imag = im * turns[0] - re * turns[1]
            sides[0].append(
                jnp.concatenate([real[:half] + real[half:], imag[:half] - imag[half:]], axis=0)
            )
            sides[1].append(
                jnp.concatenate([real[:half] - real[half:], imag[:half] + imag[half:]], axis=0)
            )
        results = []
        for parity in range(2):
            high, low = parts_of(jnp.concatenate(sides[parity], axis=1))
            results.append(
                dot(join[parity, 0], high) + dot(join[parity, 0], low) + dot(join[parity, 1], high)
            )
        return results

    def turned_product(left, right):
        lr, li = left[:, :LANES], left[:, LANES:]
        rr, ri = right[:, :LANES], right[:, LANES:]
        return jnp.concatenate([lr * rr + li * ri, lr * ri - li * rr], axis=1)

    def cut(sides):
        return [
            sides[m % 2][
                (m // 2) * seq_count : (m // 2 + 1) * seq_count, c * LANES : (c + 1) * LANES
            ]
            for c in range(own)
            for m in range(pieces)
        ]

    def encode(values, inverse):
        scaled = values * (1.0 / inverse)
        square = scaled * scaled
        fourth = square * square
        return (fourth * fourth * scaled).astype(BF16)

    def decode(coded, inverse):
        values = coded.astype(F32)
        size = jnp.abs(values)
        root = jnp.exp2(jnp.log2(size) * (1.0 / POWER)) * inverse
        root = jnp.where(size > 0.0, root, 0.0)
        return jnp.where(values < 0.0, -root, root)

    arrive(recv_t, seq_count - 1, 0)
    gather(recv_t[...], 1, 0)
    arrive(recv_c, total - 1, 1)
    for side in range(trace_groups):
        gather(recv_c[side * seq_count : (side + 1) * seq_count], held, 1 + side * held)
    lax.fori_loop(0, 1 + traces, ahead_item, 0)

    arrive(peaks_far, far_count - 1, 6)
    bounds = jnp.max(peaks_far[...], axis=0)

    def bound(position):
        return jnp.max(jnp.where(lane == position, bounds, 0.0), axis=1, keepdims=True)

    reach = math.sqrt(seq_count * span) / CEILING
    inverse_i = jnp.maximum(bound(0) * bound(1) * reach, 2.0**-120)
    inverse_f = jnp.maximum(bound(0) * bound(2) * (reach * traces), 2.0**-120)

    def input_group(side, carry):
        listed = []
        for i in range(held):
            n = 1 + side * held + i
            sides = back_item([turned_product(spectra[0, c], spectra[n, c]) for c in range(own)])
            listed += cut([encode(values, inverse_i) for values in sides])
        base = pl.multiple_of(side * seq_count, seq_count)
        out_i[pl.ds(base, seq_count)] = jnp.swapaxes(jnp.stack(listed), 0, 1)

        def send_input(step, carry):
            target = side * seq_count + lax.rem(seq + step * STRIDE, seq_count)

            @pl.when(target != me)
            def _():
                push(out_i.at[target], in_i.at[me], 3, target)

            return carry

        lax.fori_loop(0, seq_count, send_input, 0)
        return carry

    lax.fori_loop(0, trace_groups, input_group, 0)
    in_i[me] = out_i[me]

    arrive(recv_s, total - 1, 2)
    for side in range(trace_groups):
        gather(recv_s[side * seq_count : (side + 1) * seq_count], held, 1 + traces + side * held)
    lax.fori_loop(1 + traces, 1 + 2 * traces, ahead_item, 0)
    sums = []
    for c in range(own):
        acc = None
        for b in range(traces):
            product = turned_product(spectra[1 + traces + b, c], spectra[1 + b, c])
            acc = product if acc is None else acc + product
        sums.append(acc)
    coded = cut([encode(values, inverse_f) for values in back_item(sums)])
    out_f[...] = jnp.swapaxes(jnp.stack(coded), 0, 1)
    in_f[me] = out_f[seq]

    def send_filter(step, carry):
        push(out_f.at[lax.rem(other(step), seq_count)], in_f.at[me], 4, other(step))
        return carry

    lax.fori_loop(1, total, send_filter, 0)

    arrive(in_i, total - 1, 3)
    moved = jnp.swapaxes(in_i[...], 0, 1)
    for i in range(held):
        for c in range(own):
            for m in range(pieces):
                done_i[i, m * LANES : (m + 1) * LANES, c * total : (c + 1) * total] = decode(
                    moved[(i * own + c) * pieces + m], inverse_i
                ).T
    store_i = pltpu.make_async_copy(done_i, input_out, store_sem.at[0])
    store_i.start()
    arrive(in_f, total - 1, 4)
    moved = jnp.swapaxes(in_f[...], 0, 1)
    for c in range(own):
        for m in range(pieces):
            done_f[m * LANES : (m + 1) * LANES, c * total : (c + 1) * total] = decode(
                moved[c * pieces + m], inverse_f
            ).T
    store_f = pltpu.make_async_copy(done_f, filter_out, store_sem.at[1])
    store_f.start()
    depart(recv_t, seq_count - 1, 0)
    depart(recv_c, total - 1, 1)
    depart(recv_s, total - 1, 2)
    depart(in_i, total - 1, 3)
    depart(in_f, total - 1, 4)
    depart(peaks_near, near_count - 1, 5)
    depart(peaks_far, far_count - 1, 6)
    store_i.wait()
    store_f.wait()


def local(seq_count, trace_groups, signal, cotangent, filter_taps):
    total = seq_count * trace_groups
    held, span, channels = signal.shape
    own = channels // total
    pieces = span // LANES
    rows = seq_count * pieces
    items = 1 + 2 * held * trace_groups
    near_count = min(16, total // 2)
    constants = [jnp.asarray(table) for table in tables(seq_count, pieces)]
    wide, thin = held * own * pieces, own * pieces
    inputs = [cotangent, filter_taps, signal, *constants]
    anywhere = pl.BlockSpec(memory_space=pl.ANY)

    def body(*refs):
        kernel(seq_count, trace_groups, near_count, *refs)

    return pl.pallas_call(
        body,
        out_shape=(
            jax.ShapeDtypeStruct((held, span, channels), F32),
            jax.ShapeDtypeStruct((span, channels), F32),
        ),
        in_specs=[anywhere] * len(inputs),
        out_specs=(anywhere, anywhere),
        scratch_shapes=[pltpu.VMEM(array.shape, array.dtype) for array in inputs]
        + [
            pltpu.VMEM((total, wide, LANES), BF16),
            pltpu.VMEM((total, thin, LANES), BF16),
            pltpu.VMEM((total, wide, LANES), BF16),
            pltpu.VMEM((total, wide, LANES), BF16),
            pltpu.VMEM((seq_count, thin, LANES), BF16),
            pltpu.VMEM((total, wide, LANES), BF16),
            pltpu.VMEM((1, LANES), F32),
            pltpu.VMEM((near_count, 1, LANES), F32),
            pltpu.VMEM((1, LANES), F32),
            pltpu.VMEM((total // near_count, 1, LANES), F32),
            pltpu.VMEM((items, 2, rows // 2, own * LANES), BF16),
            pltpu.VMEM((items, own, rows, 2 * LANES), F32),
            pltpu.VMEM((total, wide, LANES), BF16),
            pltpu.VMEM((seq_count, thin, LANES), BF16),
            pltpu.VMEM((total, wide, LANES), BF16),
            pltpu.VMEM((total, thin, LANES), BF16),
            pltpu.VMEM((held, span, channels), F32),
            pltpu.VMEM((span, channels), F32),
            pltpu.SemaphoreType.DMA((len(inputs),)),
            pltpu.SemaphoreType.DMA((2,)),
            pltpu.SemaphoreType.DMA((7,)),
            pltpu.SemaphoreType.DMA((7,)),
        ],
        name="correlate",
        compiler_params=pltpu.CompilerParams(
            collective_id=0, has_side_effects=True, vmem_limit_bytes=32 << 20
        ),
    )(*[pltpu.with_memory_space_constraint(x, pltpu.HBM) for x in inputs])


def solution(mesh):
    seq_count, trace_groups = mesh.shape["seq"], mesh.shape["trace"]

    def run(signal, cotangent, filter_taps):
        return local(seq_count, trace_groups, signal, cotangent, filter_taps)

    in_specs = (P("trace", "seq", None), P("trace", "seq", None), P("seq", None))
    out_specs = (P("trace", "seq", None), P("seq", None))
    return jax.shard_map(run, mesh=mesh, in_specs=in_specs, out_specs=out_specs, check_vma=False)
```

```python
import math

import jax
import jax.numpy as jnp
import numpy as np
from jax import lax
from jax.experimental import pallas as pl
from jax.experimental.pallas import tpu as pltpu
from jax.sharding import PartitionSpec as P

LANES = 128
STRIDE = 37
POWER = 9
CEILING = 2.0**14
UNROLL = 8
LOGICAL = pl.DeviceIdType.LOGICAL
F32 = jnp.float32
BF16 = jnp.bfloat16


def halves(values):
    high = np.asarray(values, np.float32).astype(jnp.bfloat16)
    low = (values - high.astype(np.float64)).astype(jnp.bfloat16)
    return high, low


def tables(seq_count, pieces):
    rows = seq_count * pieces
    length = rows * LANES
    near = np.arange(rows // 2) + 0.5
    odd = np.concatenate([near, rows - near])
    scale = (2.0 / (2 * length)) / math.sqrt(length)
    splits, joins = [], []
    for parity in range(2):
        order = np.concatenate(
            [np.arange(seq_count) * pieces + m for m in range(parity, pieces, 2)]
        )
        angle = 2.0 * math.pi * near[:, None] * order[None, :] / (2 * rows)
        high, low = halves(np.concatenate([np.cos(angle), -np.sin(angle)], axis=0))
        splits.append(np.concatenate([high, low], axis=1))
        joins.append(
            np.stack(halves(np.concatenate([np.cos(angle.T), -np.sin(angle.T)], axis=1) * scale))
        )
    turn = 2.0 * math.pi * odd[:, None] * np.arange(LANES)[None, :] / (2 * length)
    inner = 2.0 * math.pi * np.outer(np.arange(LANES), np.arange(LANES)) / LANES
    cos, sin = np.cos(inner), np.sin(inner)
    ahead = np.block([[cos, -sin], [sin, cos]])
    back = np.block([[cos, sin], [-sin, cos]])
    turns = np.stack([np.cos(turn), -np.sin(turn)]).astype(np.float32)
    return np.stack(splits), np.stack(joins), np.stack(halves(ahead)), np.stack(halves(back)), turns


def parts_of(values):
    high = values.astype(BF16)
    return high, (values - high.astype(F32)).astype(BF16)


def dot(left, right):
    return jnp.dot(left, right, preferred_element_type=F32)


def sweep(start, stop, action):
    groups = (stop - start) // UNROLL

    def batch(index, carry):
        for k in range(UNROLL):
            action(start + index * UNROLL + k)
        return carry

    lax.fori_loop(0, groups, batch, 0)
    for step in range(start + groups * UNROLL, stop):
        action(step)


def kernel(seq_count, trace_groups, near_count, cot_h, taps_h, sig_h, split_h, join_h, ahead_h,
           back_h, turns_h, input_out, filter_out, cot, taps, sig, split, join, ahead, back, turns,
           send_c, send_t, send_s, recv_c, recv_t, recv_s, peak, peaks_near, peak_far, peaks_far,
           sequences, spectra, out_i, out_f, in_i, in_f, done_i, done_f,
           load_sem, store_sem, send_sem, recv_sem):
    total = seq_count * trace_groups
    held, span, channels = cot.shape
    own = channels // total
    pieces = span // LANES
    traces = held * trace_groups
    rows = seq_count * pieces
    half = rows // 2
    far_count = total // near_count
    seq = lax.axis_index("seq")
    group = lax.axis_index("trace")
    me = seq * trace_groups + group
    barrier = pltpu.get_barrier_semaphore()

    loads = [
        pltpu.make_async_copy(src, dst, load_sem.at[n])
        for n, (src, dst) in enumerate(
            [(cot_h, cot), (taps_h, taps), (sig_h, sig), (split_h, split), (join_h, join),
             (ahead_h, ahead), (back_h, back), (turns_h, turns)]
        )
    ]
    for copy in loads:
        copy.start()

    def other(step):
        return lax.rem(me + step * STRIDE, total)

    def along(step):
        return lax.rem(seq + step * STRIDE, seq_count)

    sweep(1, total, lambda step: pl.semaphore_signal(
        barrier, inc=1, device_id=other(step), device_id_type=LOGICAL))

    def spread(block):
        turned = block.T
        listed = [
            turned[c * total : (c + 1) * total, m * LANES : (m + 1) * LANES]
            for c in range(own)
            for m in range(pieces)
        ]
        return jnp.swapaxes(jnp.stack(listed), 0, 1)

    def largest(values):
        return jnp.max(jnp.abs(values.astype(F32)))

    for copy in loads[:3]:
        copy.wait()
    send_t[...] = spread(taps[...])
    recv_t[seq] = send_t[me]
    for i in range(held):
        send_c[i] = spread(cot[i])
        recv_c[i, me] = send_c[i, me]
        send_s[i] = spread(sig[i])
        recv_s[i, me] = send_s[i, me]
    lane = lax.broadcasted_iota(jnp.int32, (1, LANES), 1)
    peak[...] = jnp.where(
        lane == 0, largest(cot[...]), jnp.where(lane == 1, largest(taps[...]), largest(sig[...]))
    )
    first = lax.div(me, near_count)
    second = lax.rem(me, near_count)
    peaks_near[second] = peak[...]
    pl.semaphore_wait(barrier, total - 1)

    def push(source, target, slot, device):
        pltpu.make_async_remote_copy(
            src_ref=source,
            dst_ref=target,
            send_sem=send_sem.at[slot],
            recv_sem=recv_sem.at[slot],
            device_id=device,
            device_id_type=LOGICAL,
        ).start()

    def arrive(ref, count, slot):
        view = ref.at[pl.ds(0, count)]
        pltpu.make_async_copy(view, view, recv_sem.at[slot]).wait()

    def depart(ref, count, slot):
        view = ref.at[pl.ds(0, count)]
        pltpu.make_async_copy(view, view, send_sem.at[slot]).wait()

    taps_slot, near_slot, far_slot, filter_slot, input_slot = range(5)
    cot_slot = 5
    sig_slot = 5 + held

    def send_near(step):
        push(peak, peaks_near.at[second], near_slot,
             first * near_count + lax.rem(second + step, near_count))

    def send_far(step):
        push(peak_far, peaks_far.at[first], far_slot,
             lax.rem(first + step, far_count) * near_count + second)

    def send_taps(step):
        target = along(step) * trace_groups + group
        push(send_t.at[target], recv_t.at[seq], taps_slot, target)

    def send_cot(i):
        return lambda step: push(
            send_c.at[i, other(step)], recv_c.at[i, me], cot_slot + i, other(step))

    def send_sig(i):
        return lambda step: push(
            send_s.at[i, other(step)], recv_s.at[i, me], sig_slot + i, other(step))

    sweep(1, near_count, send_near)
    sweep(1, seq_count, send_taps)
    for i in range(held):
        sweep(1, total, send_cot(i))
    arrive(peaks_near, near_count - 1, near_slot)
    peak_far[...] = jnp.max(peaks_near[...], axis=0)
    peaks_far[first] = peak_far[...]
    sweep(1, far_count, send_far)
    for i in range(held):
        sweep(1, total, send_sig(i))
    for copy in loads[3:]:
        copy.wait()

    def gather(block, item):
        moved = jnp.swapaxes(block, 0, 1)
        for parity in range(2):
            columns = [
                jnp.concatenate([moved[c * pieces + m] for m in range(parity, pieces, 2)], axis=0)
                for c in range(own)
            ]
            sequences[item, parity] = jnp.concatenate(columns, axis=1)

    def gather_groups(blocks, item):
        blocks = blocks.reshape((seq_count, trace_groups) + blocks.shape[1:])
        for side in range(trace_groups):
            gather(blocks[:, side], item + side)

    def ahead_first(n):
        sides = []
        for parity in range(2):
            values = sequences[n, parity]
            sides.append(dot(split[parity], jnp.concatenate([values, values], axis=0)))
        even_re, even_im = sides[0][:half], sides[0][half:]
        odd_re, odd_im = sides[1][:half], sides[1][half:]
        real = jnp.concatenate([even_re + odd_re, even_re - odd_re], axis=0)
        imag = jnp.concatenate([even_im + odd_im, odd_im - even_im], axis=0)
        listed = []
        for c in range(own):
            lanes = slice(c * LANES, (c + 1) * LANES)
            re, im = real[:, lanes], imag[:, lanes]
            listed.append(parts_of(jnp.concatenate(
                [re * turns[0] - im * turns[1], re * turns[1] + im * turns[0]], axis=1
            )))
        return listed

    def ahead_second(n, listed):
        for c, (high, low) in enumerate(listed):
            spectra[n, c] = dot(high, ahead[0]) + dot(low, ahead[0]) + dot(high, ahead[1])

    def ahead_all(start, stop):
        waiting = ahead_first(start)
        for n in range(start, stop):
            following = ahead_first(n + 1) if n + 1 < stop else None
            ahead_second(n, waiting)
            waiting = following

    def back_item(products):
        sides = [[], []]
        for product in products:
            high, low = parts_of(product)
            mid = dot(high, back[0]) + dot(low, back[0]) + dot(high, back[1])
            re, im = mid[:, :LANES], mid[:, LANES:]
            real = re * turns[0] + im * turns[1]
            imag = im * turns[0] - re * turns[1]
            sides[0].append(
                jnp.concatenate([real[:half] + real[half:], imag[:half] - imag[half:]], axis=0)
            )
            sides[1].append(
                jnp.concatenate([real[:half] - real[half:], imag[:half] + imag[half:]], axis=0)
            )
        results = []
        for parity in range(2):
            high, low = parts_of(jnp.concatenate(sides[parity], axis=1))
            results.append(
                dot(join[parity, 0], high) + dot(join[parity, 0], low) + dot(join[parity, 1], high)
            )
        return results

    def turned_product(left, right):
        lr, li = left[:, :LANES], left[:, LANES:]
        rr, ri = right[:, :LANES], right[:, LANES:]
        return jnp.concatenate([lr * rr + li * ri, lr * ri - li * rr], axis=1)

    def cut(sides):
        return [
            sides[m % 2][
                (m // 2) * seq_count : (m // 2 + 1) * seq_count, c * LANES : (c + 1) * LANES
            ]
            for c in range(own)
            for m in range(pieces)
        ]

    def encode(values, inverse):
        scaled = values * (1.0 / inverse)
        square = scaled * scaled
        fourth = square * square
        return (fourth * fourth * scaled).astype(BF16)

    def decode(coded, inverse):
        values = coded.astype(F32)
        size = jnp.abs(values)
        root = jnp.exp2(jnp.log2(size) * (1.0 / POWER)) * inverse
        root = jnp.where(size > 0.0, root, 0.0)
        return jnp.where(values < 0.0, -root, root)

    first_c, first_s = 1, 1 + traces
    arrive(recv_t, seq_count - 1, taps_slot)
    gather(recv_t[...], 0)
    for i in range(held):
        arrive(recv_c.at[i], total - 1, cot_slot + i)
        base = first_c + i * trace_groups
        gather_groups(recv_c[i], base)
        ahead_all(base if i else 0, base + trace_groups)

    arrive(peaks_far, far_count - 1, far_slot)
    bounds = jnp.max(peaks_far[...], axis=0)

    def bound(position):
        return jnp.max(jnp.where(lane == position, bounds, 0.0), axis=1, keepdims=True)

    reach = math.sqrt(seq_count * span) / CEILING
    inverse_i = jnp.maximum(bound(0) * bound(1) * reach, 2.0**-120)
    inverse_f = jnp.maximum(bound(0) * bound(2) * (reach * traces), 2.0**-120)

    for turn in range(trace_groups):
        side = lax.rem(group + 1 + turn, trace_groups)
        listed = []
        for i in range(held):
            n = first_c + i * trace_groups + side
            sides = back_item([turned_product(spectra[0, c], spectra[n, c]) for c in range(own)])
            listed += cut([encode(values, inverse_i) for values in sides])
        out_i[:, side] = jnp.swapaxes(jnp.stack(listed), 0, 1)

        def send_input(step):
            target = along(step)
            push(out_i.at[target, side], in_i.at[me], input_slot, target * trace_groups + side)

        sweep(1 if turn == trace_groups - 1 else 0, seq_count, send_input)
    in_i[me] = out_i[seq, group]

    for i in range(held):
        arrive(recv_s.at[i], total - 1, sig_slot + i)
        base = first_s + i * trace_groups
        gather_groups(recv_s[i], base)
        ahead_all(base, base + trace_groups)
    sums = []
    for c in range(own):
        acc = None
        for b in range(traces):
            product = turned_product(spectra[first_s + b, c], spectra[first_c + b, c])
            acc = product if acc is None else acc + product
        sums.append(acc)
    coded = cut([encode(values, inverse_f) for values in back_item(sums)])
    out_f[...] = jnp.swapaxes(jnp.stack(coded), 0, 1)
    in_f[me] = out_f[seq]
    sweep(1, total, lambda step: push(
        out_f.at[lax.div(other(step), trace_groups)], in_f.at[me], filter_slot, other(step)))

    arrive(in_i, total - 1, input_slot)
    moved = jnp.swapaxes(in_i[...], 0, 1)
    for i in range(held):
        for c in range(own):
            for m in range(pieces):
                done_i[i, m * LANES : (m + 1) * LANES, c * total : (c + 1) * total] = decode(
                    moved[(i * own + c) * pieces + m], inverse_i
                ).T
    store_i = pltpu.make_async_copy(done_i, input_out, store_sem.at[0])
    store_i.start()
    arrive(in_f, total - 1, filter_slot)
    moved = jnp.swapaxes(in_f[...], 0, 1)
    for c in range(own):
        for m in range(pieces):
            done_f[m * LANES : (m + 1) * LANES, c * total : (c + 1) * total] = decode(
                moved[c * pieces + m], inverse_f
            ).T
    store_f = pltpu.make_async_copy(done_f, filter_out, store_sem.at[1])
    store_f.start()
    depart(recv_t, seq_count - 1, taps_slot)
    for i in range(held):
        depart(recv_c.at[i], total - 1, cot_slot + i)
        depart(recv_s.at[i], total - 1, sig_slot + i)
    depart(in_i, total - 1, input_slot)
    depart(in_f, total - 1, filter_slot)
    depart(peaks_near, near_count - 1, near_slot)
    depart(peaks_far, far_count - 1, far_slot)
    store_i.wait()
    store_f.wait()


def local(seq_count, trace_groups, signal, cotangent, filter_taps):
    total = seq_count * trace_groups
    held, span, channels = signal.shape
    own = channels // total
    pieces = span // LANES
    rows = seq_count * pieces
    items = 1 + 2 * held * trace_groups
    near_count = min(16, total // 2)
    constants = [jnp.asarray(table) for table in tables(seq_count, pieces)]
    wide, thin = held * own * pieces, own * pieces
    inputs = [cotangent, filter_taps, signal, *constants]
    anywhere = pl.BlockSpec(memory_space=pl.ANY)

    def body(*refs):
        kernel(seq_count, trace_groups, near_count, *refs)

    return pl.pallas_call(
        body,
        out_shape=(
            jax.ShapeDtypeStruct((held, span, channels), F32),
            jax.ShapeDtypeStruct((span, channels), F32),
        ),
        in_specs=[anywhere] * len(inputs),
        out_specs=(anywhere, anywhere),
        scratch_shapes=[pltpu.VMEM(array.shape, array.dtype) for array in inputs]
        + [
            pltpu.VMEM((held, total, thin, LANES), BF16),
            pltpu.VMEM((total, thin, LANES), BF16),
            pltpu.VMEM((held, total, thin, LANES), BF16),
            pltpu.VMEM((held, total, thin, LANES), BF16),
            pltpu.VMEM((seq_count, thin, LANES), BF16),
            pltpu.VMEM((held, total, thin, LANES), BF16),
            pltpu.VMEM((1, LANES), F32),
            pltpu.VMEM((near_count, 1, LANES), F32),
            pltpu.VMEM((1, LANES), F32),
            pltpu.VMEM((total // near_count, 1, LANES), F32),
            pltpu.VMEM((items, 2, rows // 2, own * LANES), BF16),
            pltpu.VMEM((items, own, rows, 2 * LANES), F32),
            pltpu.VMEM((seq_count, trace_groups, wide, LANES), BF16),
            pltpu.VMEM((seq_count, thin, LANES), BF16),
            pltpu.VMEM((total, wide, LANES), BF16),
            pltpu.VMEM((total, thin, LANES), BF16),
            pltpu.VMEM((held, span, channels), F32),
            pltpu.VMEM((span, channels), F32),
            pltpu.SemaphoreType.DMA((len(inputs),)),
            pltpu.SemaphoreType.DMA((2,)),
            pltpu.SemaphoreType.DMA((5 + 2 * held,)),
            pltpu.SemaphoreType.DMA((5 + 2 * held,)),
        ],
        name="correlate",
        compiler_params=pltpu.CompilerParams(
            collective_id=0, has_side_effects=True, vmem_limit_bytes=32 << 20
        ),
    )(*[pltpu.with_memory_space_constraint(x, pltpu.HBM) for x in inputs])


def solution(mesh):
    seq_count, trace_groups = mesh.shape["seq"], mesh.shape["trace"]

    def run(signal, cotangent, filter_taps):
        return local(seq_count, trace_groups, signal, cotangent, filter_taps)

    in_specs = (P("trace", "seq", None), P("trace", "seq", None), P("seq", None))
    out_specs = (P("trace", "seq", None), P("seq", None))
    return jax.shard_map(run, mesh=mesh, in_specs=in_specs, out_specs=out_specs, check_vma=False)
```

```python
import math

import jax
import jax.numpy as jnp
import numpy as np
from jax import lax
from jax.experimental import pallas as pl
from jax.experimental.pallas import tpu as pltpu
from jax.sharding import PartitionSpec as P

LANES = 128
STRIDE = 37
POWER = 9
CEILING = 2.0**14
UNROLL = 8
COT_PARTS = 2
SIG_PARTS = 1
LOGICAL = pl.DeviceIdType.LOGICAL
F32 = jnp.float32
BF16 = jnp.bfloat16


def halves(values):
    high = np.asarray(values, np.float32).astype(jnp.bfloat16)
    low = (values - high.astype(np.float64)).astype(jnp.bfloat16)
    return high, low


def tables(seq_count, pieces):
    rows = seq_count * pieces
    length = rows * LANES
    near = np.arange(rows // 2) + 0.5
    odd = np.concatenate([near, rows - near])
    scale = (2.0 / (2 * length)) / math.sqrt(length)
    splits, joins = [], []
    for parity in range(2):
        order = np.concatenate(
            [np.arange(seq_count) * pieces + m for m in range(parity, pieces, 2)]
        )
        angle = 2.0 * math.pi * near[:, None] * order[None, :] / (2 * rows)
        high, low = halves(np.concatenate([np.cos(angle), -np.sin(angle)], axis=0))
        splits.append(np.concatenate([high, low], axis=1))
        joins.append(
            np.stack(halves(np.concatenate([np.cos(angle.T), -np.sin(angle.T)], axis=1) * scale))
        )
    turn = 2.0 * math.pi * odd[:, None] * np.arange(LANES)[None, :] / (2 * length)
    inner = 2.0 * math.pi * np.outer(np.arange(LANES), np.arange(LANES)) / LANES
    cos, sin = np.cos(inner), np.sin(inner)
    ahead = np.block([[cos, -sin], [sin, cos]])
    back = np.block([[cos, sin], [-sin, cos]])
    turns = np.stack([np.cos(turn), -np.sin(turn)]).astype(np.float32)
    return np.stack(splits), np.stack(joins), np.stack(halves(ahead)), np.stack(halves(back)), turns


def parts_of(values):
    high = values.astype(BF16)
    return high, (values - high.astype(F32)).astype(BF16)


def dot(left, right):
    return jnp.dot(left, right, preferred_element_type=F32)


def decode(coded, inverse):
    values = coded.astype(F32)
    size = jnp.abs(values)
    root = jnp.exp2(jnp.log2(size) * (1.0 / POWER)) * inverse
    root = jnp.where(size > 0.0, root, 0.0)
    return jnp.where(values < 0.0, -root, root)


def sweep(start, stop, action):
    groups = (stop - start) // UNROLL

    def batch(index, carry):
        for k in range(UNROLL):
            action(start + index * UNROLL + k)
        return carry

    lax.fori_loop(0, groups, batch, 0)
    for step in range(start + groups * UNROLL, stop):
        action(step)


def kernel(seq_count, trace_groups, near_count, cot_h, taps_h, sig_h, split_h, join_h, ahead_h,
           back_h, turns_h, input_out, in_f, scale_out, cot, taps, sig, split, join, ahead, back, turns,
           send_c, send_t, send_s, recv_c, recv_t, recv_s, peak, peaks_near, peak_far, peaks_far,
           sequences, spectra, out_i, out_f, in_i, done_i, scale,
           load_sem, store_sem, send_sem, recv_sem):
    total = seq_count * trace_groups
    held, span, channels = cot.shape
    own = channels // total
    pieces = span // LANES
    traces = held * trace_groups
    rows = seq_count * pieces
    half = rows // 2
    far_count = total // near_count
    seq = lax.axis_index("seq")
    group = lax.axis_index("trace")
    me = seq * trace_groups + group
    cot_parts, sig_parts = send_c.shape[0], send_s.shape[0]
    barrier = pltpu.get_barrier_semaphore()

    loads = [
        pltpu.make_async_copy(src, dst, load_sem.at[n])
        for n, (src, dst) in enumerate(
            [(cot_h, cot), (taps_h, taps), (sig_h, sig), (split_h, split), (join_h, join),
             (ahead_h, ahead), (back_h, back), (turns_h, turns)]
        )
    ]
    for copy in loads:
        copy.start()

    def other(step):
        return lax.rem(me + step * STRIDE, total)

    def along(step):
        return lax.rem(seq + step * STRIDE, seq_count)

    sweep(1, total, lambda step: pl.semaphore_signal(
        barrier, inc=1, device_id=other(step), device_id_type=LOGICAL))

    def part(ref, index, parts):
        step = held // parts
        return [ref[i] for i in range(index * step, (index + 1) * step)]

    def spread(blocks):
        turned = [block.T for block in blocks]
        listed = [
            block[c * total : (c + 1) * total, m * LANES : (m + 1) * LANES]
            for block in turned
            for c in range(own)
            for m in range(pieces)
        ]
        return jnp.swapaxes(jnp.stack(listed), 0, 1)

    def largest(values):
        return jnp.max(jnp.abs(values.astype(F32)))

    def push(source, target, slot, device):
        pltpu.make_async_remote_copy(
            src_ref=source,
            dst_ref=target,
            send_sem=send_sem.at[slot],
            recv_sem=recv_sem.at[slot],
            device_id=device,
            device_id_type=LOGICAL,
        ).start()

    def arrive(ref, count, slot):
        view = ref.at[pl.ds(0, count)]
        pltpu.make_async_copy(view, view, recv_sem.at[slot]).wait()

    def depart(ref, count, slot):
        view = ref.at[pl.ds(0, count)]
        pltpu.make_async_copy(view, view, send_sem.at[slot]).wait()

    taps_slot, near_slot, far_slot, filter_slot, input_slot = range(5)
    cot_slot = 5
    sig_slot = 5 + cot_parts

    def send_near(step):
        push(peak, peaks_near.at[second], near_slot,
             first * near_count + lax.rem(second + step, near_count))

    def send_far(step):
        push(peak_far, peaks_far.at[first], far_slot,
             lax.rem(first + step, far_count) * near_count + second)

    def send_taps(step):
        target = along(step) * trace_groups + group
        push(send_t.at[target], recv_t.at[seq], taps_slot, target)

    def send_cot(i):
        return lambda step: push(
            send_c.at[i, other(step)], recv_c.at[i, me], cot_slot + i, other(step))

    def send_sig(i):
        return lambda step: push(
            send_s.at[i, other(step)], recv_s.at[i, me], sig_slot + i, other(step))

    def stage(blocks, send, receive, place):
        send[...] = spread(blocks)
        receive[place] = send[me]

    loads[1].wait()
    stage([taps[...]], send_t, recv_t, seq)
    loads[0].wait()
    stage(part(cot, 0, cot_parts), send_c.at[0], recv_c.at[0], me)
    loads[2].wait()
    lane = lax.broadcasted_iota(jnp.int32, (1, LANES), 1)
    peak[...] = jnp.where(
        lane == 0, largest(cot[...]), jnp.where(lane == 1, largest(taps[...]), largest(sig[...]))
    )
    first = lax.div(me, near_count)
    second = lax.rem(me, near_count)
    peaks_near[second] = peak[...]
    pl.semaphore_wait(barrier, total - 1)
    sweep(1, near_count, send_near)
    sweep(1, seq_count, send_taps)
    sweep(1, total, send_cot(0))
    for i in range(1, cot_parts):
        stage(part(cot, i, cot_parts), send_c.at[i], recv_c.at[i], me)
        sweep(1, total, send_cot(i))
    arrive(peaks_near, near_count - 1, near_slot)
    peak_far[...] = jnp.max(peaks_near[...], axis=0)
    peaks_far[first] = peak_far[...]
    sweep(1, far_count, send_far)
    for i in range(sig_parts):
        stage(part(sig, i, sig_parts), send_s.at[i], recv_s.at[i], me)
        sweep(1, total, send_sig(i))
    for copy in loads[3:]:
        copy.wait()

    def gather(block, items):
        moved = jnp.swapaxes(block, 0, 1)
        for i, item in enumerate(items):
            for parity in range(2):
                columns = [
                    jnp.concatenate(
                        [moved[(i * own + c) * pieces + m] for m in range(parity, pieces, 2)],
                        axis=0,
                    )
                    for c in range(own)
                ]
                sequences[item, parity] = jnp.concatenate(columns, axis=1)

    def gather_groups(blocks, start, stop):
        blocks = blocks.reshape((seq_count, trace_groups) + blocks.shape[1:])
        for side in range(trace_groups):
            gather(blocks[:, side], range(start + side, stop, trace_groups))

    def ahead_first(n):
        sides = []
        for parity in range(2):
            values = sequences[n, parity]
            sides.append(dot(split[parity], jnp.concatenate([values, values], axis=0)))
        even_re, even_im = sides[0][:half], sides[0][half:]
        odd_re, odd_im = sides[1][:half], sides[1][half:]
        real = jnp.concatenate([even_re + odd_re, even_re - odd_re], axis=0)
        imag = jnp.concatenate([even_im + odd_im, odd_im - even_im], axis=0)
        listed = []
        for c in range(own):
            lanes = slice(c * LANES, (c + 1) * LANES)
            re, im = real[:, lanes], imag[:, lanes]
            listed.append(parts_of(jnp.concatenate(
                [re * turns[0] - im * turns[1], re * turns[1] + im * turns[0]], axis=1
            )))
        return listed

    def ahead_second(n, listed):
        for c, (high, low) in enumerate(listed):
            spectra[n, c] = dot(high, ahead[0]) + dot(low, ahead[0]) + dot(high, ahead[1])

    def ahead_all(start, stop):
        waiting = ahead_first(start)
        for n in range(start, stop):
            following = ahead_first(n + 1) if n + 1 < stop else None
            ahead_second(n, waiting)
            waiting = following

    def back_item(products):
        sides = [[], []]
        for product in products:
            high, low = parts_of(product)
            mid = dot(high, back[0]) + dot(low, back[0]) + dot(high, back[1])
            re, im = mid[:, :LANES], mid[:, LANES:]
            real = re * turns[0] + im * turns[1]
            imag = im * turns[0] - re * turns[1]
            sides[0].append(
                jnp.concatenate([real[:half] + real[half:], imag[:half] - imag[half:]], axis=0)
            )
            sides[1].append(
                jnp.concatenate([real[:half] - real[half:], imag[:half] + imag[half:]], axis=0)
            )
        results = []
        for parity in range(2):
            high, low = parts_of(jnp.concatenate(sides[parity], axis=1))
            results.append(
                dot(join[parity, 0], high) + dot(join[parity, 0], low) + dot(join[parity, 1], high)
            )
        return results

    def turned_product(left, right):
        lr, li = left[:, :LANES], left[:, LANES:]
        rr, ri = right[:, :LANES], right[:, LANES:]
        return jnp.concatenate([lr * rr + li * ri, lr * ri - li * rr], axis=1)

    def cut(sides):
        return [
            sides[m % 2][
                (m // 2) * seq_count : (m // 2 + 1) * seq_count, c * LANES : (c + 1) * LANES
            ]
            for c in range(own)
            for m in range(pieces)
        ]

    def encode(values, inverse):
        scaled = values * (1.0 / inverse)
        square = scaled * scaled
        fourth = square * square
        return (fourth * fourth * scaled).astype(BF16)

    first_c, first_s = 1, 1 + traces
    arrive(recv_t, seq_count - 1, taps_slot)
    gather(recv_t[...], [0])
    step = traces // cot_parts
    for i in range(cot_parts):
        arrive(recv_c.at[i], total - 1, cot_slot + i)
        base = first_c + i * step
        gather_groups(recv_c[i], base, base + step)
        ahead_all(base if i else 0, base + step)

    arrive(peaks_far, far_count - 1, far_slot)
    bounds = jnp.max(peaks_far[...], axis=0)

    def bound(position):
        return jnp.max(jnp.where(lane == position, bounds, 0.0), axis=1, keepdims=True)

    reach = math.sqrt(seq_count * span) / CEILING
    inverse_i = jnp.maximum(bound(0) * bound(1) * reach, 2.0**-120)
    inverse_f = jnp.maximum(bound(0) * bound(2) * (reach * traces), 2.0**-120)

    for turn in range(trace_groups):
        side = lax.rem(group + 1 + turn, trace_groups)
        listed = []
        for i in range(held):
            n = first_c + i * trace_groups + side
            sides = back_item([turned_product(spectra[0, c], spectra[n, c]) for c in range(own)])
            listed += cut([encode(values, inverse_i) for values in sides])
        out_i[:, side] = jnp.swapaxes(jnp.stack(listed), 0, 1)

        def send_input(step):
            target = along(step)
            push(out_i.at[target, side], in_i.at[me], input_slot, target * trace_groups + side)

        sweep(1 if turn == trace_groups - 1 else 0, seq_count, send_input)
    in_i[me] = out_i[seq, group]

    sums = [None] * own
    step = traces // sig_parts
    for i in range(sig_parts):
        arrive(recv_s.at[i], total - 1, sig_slot + i)
        base = i * step
        gather_groups(recv_s[i], first_s + base, first_s + base + step)
        ahead_all(first_s + base, first_s + base + step)
        for b in range(base, base + step):
            for c in range(own):
                product = turned_product(spectra[first_s + b, c], spectra[first_c + b, c])
                sums[c] = product if sums[c] is None else sums[c] + product
    coded = cut([encode(values, inverse_f) for values in back_item(sums)])
    out_f[...] = jnp.swapaxes(jnp.stack(coded), 0, 1)
    keep = pltpu.make_async_copy(out_f.at[seq], in_f.at[me], store_sem.at[1])
    keep.start()
    scale[...] = jnp.broadcast_to(inverse_f, scale.shape)
    store_s = pltpu.make_async_copy(scale, scale_out, store_sem.at[2])
    store_s.start()
    sweep(1, total, lambda step: push(
        out_f.at[lax.div(other(step), trace_groups)], in_f.at[me], filter_slot, other(step)))

    arrive(in_i, total - 1, input_slot)
    moved = jnp.swapaxes(in_i[...], 0, 1)
    for i in range(held):
        for c in range(own):
            for m in range(pieces):
                done_i[i, m * LANES : (m + 1) * LANES, c * total : (c + 1) * total] = decode(
                    moved[(i * own + c) * pieces + m], inverse_i
                ).T
    store_i = pltpu.make_async_copy(done_i, input_out, store_sem.at[0])
    store_i.start()
    arrive(in_f, total - 1, filter_slot)
    depart(recv_t, seq_count - 1, taps_slot)
    for i in range(cot_parts):
        depart(recv_c.at[i], total - 1, cot_slot + i)
    for i in range(sig_parts):
        depart(recv_s.at[i], total - 1, sig_slot + i)
    depart(in_i, total - 1, input_slot)
    depart(in_f, total - 1, filter_slot)
    depart(peaks_near, near_count - 1, near_slot)
    depart(peaks_far, far_count - 1, far_slot)
    store_i.wait()
    keep.wait()
    store_s.wait()


def finish(input_grad, coded, scale, input_out, filter_out, done, store_sem):
    span, channels = filter_out.shape
    total = coded.shape[0]
    pieces = span // LANES
    store_i = pltpu.make_async_copy(input_grad, input_out, store_sem.at[0])
    store_i.start()
    moved = jnp.swapaxes(coded[...], 0, 1)
    stores = [store_i]
    for m in range(pieces):
        rows = pl.ds(m * LANES, LANES)
        for c in range(channels // total):
            done[rows, c * total : (c + 1) * total] = decode(moved[c * pieces + m], scale[...]).T
        stores.append(
            pltpu.make_async_copy(done.at[rows], filter_out.at[rows], store_sem.at[1 + m])
        )
        stores[-1].start()
    for store in stores:
        store.wait()


def local(seq_count, trace_groups, signal, cotangent, filter_taps):
    total = seq_count * trace_groups
    held, span, channels = signal.shape
    own = channels // total
    pieces = span // LANES
    rows = seq_count * pieces
    items = 1 + 2 * held * trace_groups
    near_count = min(16, total // 2)
    constants = [jnp.asarray(table) for table in tables(seq_count, pieces)]
    wide, thin = held * own * pieces, own * pieces
    cot_shape = (COT_PARTS, total, wide // COT_PARTS, LANES)
    sig_shape = (SIG_PARTS, total, wide // SIG_PARTS, LANES)
    inputs = [cotangent, filter_taps, signal, *constants]
    anywhere = pl.BlockSpec(memory_space=pl.ANY)

    def body(*refs):
        kernel(seq_count, trace_groups, near_count, *refs)

    input_grad, coded, scale = pl.pallas_call(
        body,
        out_shape=(
            jax.ShapeDtypeStruct((held, span, channels), F32),
            jax.ShapeDtypeStruct((total, thin, LANES), BF16),
            jax.ShapeDtypeStruct((1, LANES), F32),
        ),
        in_specs=[anywhere] * len(inputs),
        out_specs=(anywhere,) * 3,
        scratch_shapes=[pltpu.VMEM(array.shape, array.dtype) for array in inputs]
        + [
            pltpu.VMEM(cot_shape, BF16),
            pltpu.VMEM((total, thin, LANES), BF16),
            pltpu.VMEM(sig_shape, BF16),
            pltpu.VMEM(cot_shape, BF16),
            pltpu.VMEM((seq_count, thin, LANES), BF16),
            pltpu.VMEM(sig_shape, BF16),
            pltpu.VMEM((1, LANES), F32),
            pltpu.VMEM((near_count, 1, LANES), F32),
            pltpu.VMEM((1, LANES), F32),
            pltpu.VMEM((total // near_count, 1, LANES), F32),
            pltpu.VMEM((items, 2, rows // 2, own * LANES), BF16),
            pltpu.VMEM((items, own, rows, 2 * LANES), F32),
            pltpu.VMEM((seq_count, trace_groups, wide, LANES), BF16),
            pltpu.VMEM((seq_count, thin, LANES), BF16),
            pltpu.VMEM((total, wide, LANES), BF16),
            pltpu.VMEM((held, span, channels), F32),
            pltpu.VMEM((1, LANES), F32),
            pltpu.SemaphoreType.DMA((len(inputs),)),
            pltpu.SemaphoreType.DMA((3,)),
            pltpu.SemaphoreType.DMA((5 + COT_PARTS + SIG_PARTS,)),
            pltpu.SemaphoreType.DMA((5 + COT_PARTS + SIG_PARTS,)),
        ],
        name="correlate",
        compiler_params=pltpu.CompilerParams(
            collective_id=0, has_side_effects=True, vmem_limit_bytes=32 << 20
        ),
    )(*[pltpu.with_memory_space_constraint(x, pltpu.HBM) for x in inputs])
    return pl.pallas_call(
        finish,
        out_shape=(
            jax.ShapeDtypeStruct((held, span, channels), F32),
            jax.ShapeDtypeStruct((span, channels), F32),
        ),
        in_specs=[anywhere, pl.BlockSpec(memory_space=pltpu.VMEM), pl.BlockSpec(memory_space=pltpu.VMEM)],
        out_specs=(anywhere, anywhere),
        scratch_shapes=[pltpu.VMEM((span, channels), F32), pltpu.SemaphoreType.DMA((1 + pieces,))],
        name="finish",
    )(*[pltpu.with_memory_space_constraint(x, pltpu.VMEM) for x in (input_grad, coded, scale)])


def solution(mesh):
    seq_count, trace_groups = mesh.shape["seq"], mesh.shape["trace"]

    def run(signal, cotangent, filter_taps):
        return local(seq_count, trace_groups, signal, cotangent, filter_taps)

    in_specs = (P("trace", "seq", None), P("trace", "seq", None), P("seq", None))
    out_specs = (P("trace", "seq", None), P("seq", None))
    return jax.shard_map(run, mesh=mesh, in_specs=in_specs, out_specs=out_specs, check_vma=False)
```

```python
import math

import jax
import jax.numpy as jnp
import numpy as np
from jax import lax
from jax.experimental import pallas as pl
from jax.experimental.pallas import tpu as pltpu
from jax.sharding import PartitionSpec as P

LANES = 128
STRIDE = 37
GREETING = 1
POWER = 9
CEILING = 2.0**14
UNROLL = 8
COT_PARTS = 2
SIG_PARTS = 1
LOGICAL = pl.DeviceIdType.LOGICAL
F32 = jnp.float32
BF16 = jnp.bfloat16


def halves(values):
    high = np.asarray(values, np.float32).astype(jnp.bfloat16)
    low = (values - high.astype(np.float64)).astype(jnp.bfloat16)
    return high, low


def tables(seq_count, pieces):
    rows = seq_count * pieces
    length = rows * LANES
    near = np.arange(rows // 2) + 0.5
    odd = np.concatenate([near, rows - near])
    scale = (2.0 / (2 * length)) / math.sqrt(length)
    splits, joins = [], []
    for parity in range(2):
        order = np.concatenate(
            [np.arange(seq_count) * pieces + m for m in range(parity, pieces, 2)]
        )
        angle = 2.0 * math.pi * near[:, None] * order[None, :] / (2 * rows)
        high, low = halves(np.concatenate([np.cos(angle), -np.sin(angle)], axis=0))
        splits.append(np.concatenate([high, low], axis=1))
        joins.append(
            np.stack(halves(np.concatenate([np.cos(angle.T), -np.sin(angle.T)], axis=1) * scale))
        )
    turn = 2.0 * math.pi * odd[:, None] * np.arange(LANES)[None, :] / (2 * length)
    inner = 2.0 * math.pi * np.outer(np.arange(LANES), np.arange(LANES)) / LANES
    cos, sin = np.cos(inner), np.sin(inner)
    ahead = np.block([[cos, -sin], [sin, cos]])
    back = np.block([[cos, sin], [-sin, cos]])
    turns = np.stack([np.cos(turn), -np.sin(turn)]).astype(np.float32)
    return np.stack(splits), np.stack(joins), np.stack(halves(ahead)), np.stack(halves(back)), turns


def parts_of(values):
    high = values.astype(BF16)
    return high, (values - high.astype(F32)).astype(BF16)


def dot(left, right):
    return jnp.dot(left, right, preferred_element_type=F32)


def decode(coded, inverse):
    values = coded.astype(F32)
    size = jnp.abs(values)
    root = jnp.exp2(jnp.log2(size) * (1.0 / POWER)) * inverse
    root = jnp.where(size > 0.0, root, 0.0)
    return jnp.where(values < 0.0, -root, root)


def sweep(start, stop, action, unroll=UNROLL):
    groups = (stop - start) // unroll

    def batch(index, carry):
        for k in range(unroll):
            action(start + index * unroll + k)
        return carry

    lax.fori_loop(0, groups, batch, 0)
    for step in range(start + groups * unroll, stop):
        action(step)


def kernel(seq_count, trace_groups, near_count, cot_h, taps_h, sig_h, split_h, join_h, ahead_h,
           back_h, turns_h, input_out, in_f, scale_out, cot, taps, sig, split, join, ahead, back, turns,
           send_c, send_t, send_s, recv_c, recv_t, recv_s, peak, peaks_near, peak_far, peaks_far,
           sequences, spectra, out_i, out_f, in_i, done_i, scale,
           load_sem, store_sem, send_sem, recv_sem):
    total = seq_count * trace_groups
    held, span, channels = cot.shape
    own = channels // total
    pieces = span // LANES
    traces = held * trace_groups
    rows = seq_count * pieces
    half = rows // 2
    far_count = total // near_count
    seq = lax.axis_index("seq")
    group = lax.axis_index("trace")
    me = seq * trace_groups + group
    cot_parts, sig_parts = send_c.shape[0], send_s.shape[0]
    barrier = pltpu.get_barrier_semaphore()

    loads = [
        pltpu.make_async_copy(src, dst, load_sem.at[n])
        for n, (src, dst) in enumerate(
            [(cot_h, cot), (taps_h, taps), (sig_h, sig), (split_h, split), (join_h, join),
             (ahead_h, ahead), (back_h, back), (turns_h, turns)]
        )
    ]
    for copy in loads:
        copy.start()

    def other(step):
        return lax.rem(me + step * STRIDE, total)

    def along(step):
        return lax.rem(seq + step * STRIDE, seq_count)

    sweep(1, total, lambda step: pl.semaphore_signal(
        barrier, inc=1, device_id=lax.rem(me + step * GREETING, total), device_id_type=LOGICAL), 32)

    def part(ref, index, parts):
        step = held // parts
        return [ref[i] for i in range(index * step, (index + 1) * step)]

    def spread(blocks):
        turned = [block.T for block in blocks]
        listed = [
            block[c * total : (c + 1) * total, m * LANES : (m + 1) * LANES]
            for block in turned
            for c in range(own)
            for m in range(pieces)
        ]
        return jnp.swapaxes(jnp.stack(listed), 0, 1)

    def largest(values):
        return jnp.max(jnp.abs(values.astype(F32)))

    def push(source, target, slot, device):
        pltpu.make_async_remote_copy(
            src_ref=source,
            dst_ref=target,
            send_sem=send_sem.at[slot],
            recv_sem=recv_sem.at[slot],
            device_id=device,
            device_id_type=LOGICAL,
        ).start()

    def arrive(ref, count, slot):
        view = ref.at[pl.ds(0, count)]
        pltpu.make_async_copy(view, view, recv_sem.at[slot]).wait()

    def depart(ref, count, slot):
        view = ref.at[pl.ds(0, count)]
        pltpu.make_async_copy(view, view, send_sem.at[slot]).wait()

    taps_slot, near_slot, far_slot, filter_slot, input_slot = range(5)
    cot_slot = 5
    sig_slot = 5 + cot_parts

    def send_near(step):
        push(peak, peaks_near.at[second], near_slot,
             first * near_count + lax.rem(second + step, near_count))

    def send_far(step):
        push(peak_far, peaks_far.at[first], far_slot,
             lax.rem(first + step, far_count) * near_count + second)

    def send_taps(step):
        target = along(step) * trace_groups + group
        push(send_t.at[target], recv_t.at[seq], taps_slot, target)

    def send_cot(i):
        return lambda step: push(
            send_c.at[i, other(step)], recv_c.at[i, me], cot_slot + i, other(step))

    def send_sig(i):
        return lambda step: push(
            send_s.at[i, other(step)], recv_s.at[i, me], sig_slot + i, other(step))

    def stage(blocks, send, receive, place):
        send[...] = spread(blocks)
        receive[place] = send[me]

    loads[1].wait()
    stage([taps[...]], send_t, recv_t, seq)
    loads[0].wait()
    stage(part(cot, 0, cot_parts), send_c.at[0], recv_c.at[0], me)
    loads[2].wait()
    lane = lax.broadcasted_iota(jnp.int32, (1, LANES), 1)
    peak[...] = jnp.where(
        lane == 0, largest(cot[...]), jnp.where(lane == 1, largest(taps[...]), largest(sig[...]))
    )
    first = lax.div(me, near_count)
    second = lax.rem(me, near_count)
    peaks_near[second] = peak[...]
    pl.semaphore_wait(barrier, total - 1)
    sweep(1, near_count, send_near)
    sweep(1, seq_count, send_taps)
    sweep(1, total, send_cot(0))
    for i in range(1, cot_parts):
        stage(part(cot, i, cot_parts), send_c.at[i], recv_c.at[i], me)
        sweep(1, total, send_cot(i))
    arrive(peaks_near, near_count - 1, near_slot)
    peak_far[...] = jnp.max(peaks_near[...], axis=0)
    peaks_far[first] = peak_far[...]
    sweep(1, far_count, send_far)
    for i in range(sig_parts):
        stage(part(sig, i, sig_parts), send_s.at[i], recv_s.at[i], me)
        sweep(1, total, send_sig(i))
    for copy in loads[3:]:
        copy.wait()

    def gather(block, items):
        moved = jnp.swapaxes(block, 0, 1)
        for i, item in enumerate(items):
            for parity in range(2):
                columns = [
                    jnp.concatenate(
                        [moved[(i * own + c) * pieces + m] for m in range(parity, pieces, 2)],
                        axis=0,
                    )
                    for c in range(own)
                ]
                sequences[item, parity] = jnp.concatenate(columns, axis=1)

    def gather_groups(blocks, start, stop):
        blocks = blocks.reshape((seq_count, trace_groups) + blocks.shape[1:])
        for side in range(trace_groups):
            gather(blocks[:, side], range(start + side, stop, trace_groups))

    def ahead_first(n):
        sides = []
        for parity in range(2):
            values = sequences[n, parity]
            sides.append(dot(split[parity], jnp.concatenate([values, values], axis=0)))
        even_re, even_im = sides[0][:half], sides[0][half:]
        odd_re, odd_im = sides[1][:half], sides[1][half:]
        real = jnp.concatenate([even_re + odd_re, even_re - odd_re], axis=0)
        imag = jnp.concatenate([even_im + odd_im, odd_im - even_im], axis=0)
        listed = []
        for c in range(own):
            lanes = slice(c * LANES, (c + 1) * LANES)
            re, im = real[:, lanes], imag[:, lanes]
            listed.append(parts_of(jnp.concatenate(
                [re * turns[0] - im * turns[1], re * turns[1] + im * turns[0]], axis=1
            )))
        return listed

    def ahead_second(n, listed):
        for c, (high, low) in enumerate(listed):
            spectra[n, c] = dot(high, ahead[0]) + dot(low, ahead[0]) + dot(high, ahead[1])

    def ahead_all(start, stop):
        waiting = ahead_first(start)
        for n in range(start, stop):
            following = ahead_first(n + 1) if n + 1 < stop else None
            ahead_second(n, waiting)
            waiting = following

    def back_item(products):
        sides = [[], []]
        for product in products:
            high, low = parts_of(product)
            mid = dot(high, back[0]) + dot(low, back[0]) + dot(high, back[1])
            re, im = mid[:, :LANES], mid[:, LANES:]
            real = re * turns[0] + im * turns[1]
            imag = im * turns[0] - re * turns[1]
            sides[0].append(
                jnp.concatenate([real[:half] + real[half:], imag[:half] - imag[half:]], axis=0)
            )
            sides[1].append(
                jnp.concatenate([real[:half] - real[half:], imag[:half] + imag[half:]], axis=0)
            )
        results = []
        for parity in range(2):
            high, low = parts_of(jnp.concatenate(sides[parity], axis=1))
            results.append(
                dot(join[parity, 0], high) + dot(join[parity, 0], low) + dot(join[parity, 1], high)
            )
        return results

    def turned_product(left, right):
        lr, li = left[:, :LANES], left[:, LANES:]
        rr, ri = right[:, :LANES], right[:, LANES:]
        return jnp.concatenate([lr * rr + li * ri, lr * ri - li * rr], axis=1)

    def cut(sides):
        return [
            sides[m % 2][
                (m // 2) * seq_count : (m // 2 + 1) * seq_count, c * LANES : (c + 1) * LANES
            ]
            for c in range(own)
            for m in range(pieces)
        ]

    def encode(values, inverse):
        scaled = values * (1.0 / inverse)
        square = scaled * scaled
        fourth = square * square
        return (fourth * fourth * scaled).astype(BF16)

    first_c, first_s = 1, 1 + traces
    arrive(recv_t, seq_count - 1, taps_slot)
    gather(recv_t[...], [0])
    step = traces // cot_parts
    for i in range(cot_parts):
        arrive(recv_c.at[i], total - 1, cot_slot + i)
        base = first_c + i * step
        gather_groups(recv_c[i], base, base + step)
        ahead_all(base if i else 0, base + step)

    arrive(peaks_far, far_count - 1, far_slot)
    bounds = jnp.max(peaks_far[...], axis=0)

    def bound(position):
        return jnp.max(jnp.where(lane == position, bounds, 0.0), axis=1, keepdims=True)

    reach = math.sqrt(seq_count * span) / CEILING
    inverse_i = jnp.maximum(bound(0) * bound(1) * reach, 2.0**-120)
    inverse_f = jnp.maximum(bound(0) * bound(2) * (reach * traces), 2.0**-120)

    for turn in range(trace_groups):
        side = lax.rem(group + 1 + turn, trace_groups)
        listed = []
        for i in range(held):
            n = first_c + i * trace_groups + side
            sides = back_item([turned_product(spectra[0, c], spectra[n, c]) for c in range(own)])
            listed += cut([encode(values, inverse_i) for values in sides])
        out_i[:, side] = jnp.swapaxes(jnp.stack(listed), 0, 1)

        def send_input(step):
            target = along(step)
            push(out_i.at[target, side], in_i.at[me], input_slot, target * trace_groups + side)

        sweep(1 if turn == trace_groups - 1 else 0, seq_count, send_input)
    in_i[me] = out_i[seq, group]

    sums = [None] * own
    step = traces // sig_parts
    for i in range(sig_parts):
        arrive(recv_s.at[i], total - 1, sig_slot + i)
        base = i * step
        gather_groups(recv_s[i], first_s + base, first_s + base + step)
        ahead_all(first_s + base, first_s + base + step)
        for b in range(base, base + step):
            for c in range(own):
                product = turned_product(spectra[first_s + b, c], spectra[first_c + b, c])
                sums[c] = product if sums[c] is None else sums[c] + product
    coded = cut([encode(values, inverse_f) for values in back_item(sums)])
    out_f[...] = jnp.swapaxes(jnp.stack(coded), 0, 1)
    keep = pltpu.make_async_copy(out_f.at[seq], in_f.at[me], store_sem.at[1])
    keep.start()
    scale[...] = jnp.broadcast_to(inverse_f, scale.shape)
    store_s = pltpu.make_async_copy(scale, scale_out, store_sem.at[2])
    store_s.start()
    sweep(1, total, lambda step: push(
        out_f.at[lax.div(other(step), trace_groups)], in_f.at[me], filter_slot, other(step)))

    arrive(in_i, total - 1, input_slot)
    moved = jnp.swapaxes(in_i[...], 0, 1)
    for i in range(held):
        for c in range(own):
            for m in range(pieces):
                done_i[i, m * LANES : (m + 1) * LANES, c * total : (c + 1) * total] = decode(
                    moved[(i * own + c) * pieces + m], inverse_i
                ).T
    store_i = pltpu.make_async_copy(done_i, input_out, store_sem.at[0])
    store_i.start()
    arrive(in_f, total - 1, filter_slot)
    depart(recv_t, seq_count - 1, taps_slot)
    for i in range(cot_parts):
        depart(recv_c.at[i], total - 1, cot_slot + i)
    for i in range(sig_parts):
        depart(recv_s.at[i], total - 1, sig_slot + i)
    depart(in_i, total - 1, input_slot)
    depart(in_f, total - 1, filter_slot)
    depart(peaks_near, near_count - 1, near_slot)
    depart(peaks_far, far_count - 1, far_slot)
    store_i.wait()
    keep.wait()
    store_s.wait()


def finish(input_grad, coded, scale, input_out, filter_out, done, store_sem):
    span, channels = filter_out.shape
    total = coded.shape[0]
    pieces = span // LANES
    store_i = pltpu.make_async_copy(input_grad, input_out, store_sem.at[0])
    store_i.start()
    moved = jnp.swapaxes(coded[...], 0, 1)
    stores = [store_i]
    for m in range(pieces):
        rows = pl.ds(m * LANES, LANES)
        for c in range(channels // total):
            done[rows, c * total : (c + 1) * total] = decode(moved[c * pieces + m], scale[...]).T
        stores.append(
            pltpu.make_async_copy(done.at[rows], filter_out.at[rows], store_sem.at[1 + m])
        )
        stores[-1].start()
    for store in stores:
        store.wait()


def local(seq_count, trace_groups, signal, cotangent, filter_taps):
    total = seq_count * trace_groups
    held, span, channels = signal.shape
    own = channels // total
    pieces = span // LANES
    rows = seq_count * pieces
    items = 1 + 2 * held * trace_groups
    near_count = min(16, total // 2)
    constants = [jnp.asarray(table) for table in tables(seq_count, pieces)]
    wide, thin = held * own * pieces, own * pieces
    cot_shape = (COT_PARTS, total, wide // COT_PARTS, LANES)
    sig_shape = (SIG_PARTS, total, wide // SIG_PARTS, LANES)
    inputs = [cotangent, filter_taps, signal, *constants]
    anywhere = pl.BlockSpec(memory_space=pl.ANY)

    def body(*refs):
        kernel(seq_count, trace_groups, near_count, *refs)

    input_grad, coded, scale = pl.pallas_call(
        body,
        out_shape=(
            jax.ShapeDtypeStruct((held, span, channels), F32),
            jax.ShapeDtypeStruct((total, thin, LANES), BF16),
            jax.ShapeDtypeStruct((1, LANES), F32),
        ),
        in_specs=[anywhere] * len(inputs),
        out_specs=(anywhere,) * 3,
        scratch_shapes=[pltpu.VMEM(array.shape, array.dtype) for array in inputs]
        + [
            pltpu.VMEM(cot_shape, BF16),
            pltpu.VMEM((total, thin, LANES), BF16),
            pltpu.VMEM(sig_shape, BF16),
            pltpu.VMEM(cot_shape, BF16),
            pltpu.VMEM((seq_count, thin, LANES), BF16),
            pltpu.VMEM(sig_shape, BF16),
            pltpu.VMEM((1, LANES), F32),
            pltpu.VMEM((near_count, 1, LANES), F32),
            pltpu.VMEM((1, LANES), F32),
            pltpu.VMEM((total // near_count, 1, LANES), F32),
            pltpu.VMEM((items, 2, rows // 2, own * LANES), BF16),
            pltpu.VMEM((items, own, rows, 2 * LANES), F32),
            pltpu.VMEM((seq_count, trace_groups, wide, LANES), BF16),
            pltpu.VMEM((seq_count, thin, LANES), BF16),
            pltpu.VMEM((total, wide, LANES), BF16),
            pltpu.VMEM((held, span, channels), F32),
            pltpu.VMEM((1, LANES), F32),
            pltpu.SemaphoreType.DMA((len(inputs),)),
            pltpu.SemaphoreType.DMA((3,)),
            pltpu.SemaphoreType.DMA((5 + COT_PARTS + SIG_PARTS,)),
            pltpu.SemaphoreType.DMA((5 + COT_PARTS + SIG_PARTS,)),
        ],
        name="correlate",
        compiler_params=pltpu.CompilerParams(
            collective_id=0, has_side_effects=True, vmem_limit_bytes=32 << 20
        ),
    )(*[pltpu.with_memory_space_constraint(x, pltpu.HBM) for x in inputs])
    return pl.pallas_call(
        finish,
        out_shape=(
            jax.ShapeDtypeStruct((held, span, channels), F32),
            jax.ShapeDtypeStruct((span, channels), F32),
        ),
        in_specs=[anywhere, pl.BlockSpec(memory_space=pltpu.VMEM), pl.BlockSpec(memory_space=pltpu.VMEM)],
        out_specs=(anywhere, anywhere),
        scratch_shapes=[pltpu.VMEM((span, channels), F32), pltpu.SemaphoreType.DMA((1 + pieces,))],
        name="finish",
    )(*[pltpu.with_memory_space_constraint(x, pltpu.VMEM) for x in (input_grad, coded, scale)])


def solution(mesh):
    seq_count, trace_groups = mesh.shape["seq"], mesh.shape["trace"]

    def run(signal, cotangent, filter_taps):
        return local(seq_count, trace_groups, signal, cotangent, filter_taps)

    in_specs = (P("trace", "seq", None), P("trace", "seq", None), P("seq", None))
    out_specs = (P("trace", "seq", None), P("seq", None))
    return jax.shard_map(run, mesh=mesh, in_specs=in_specs, out_specs=out_specs, check_vma=False)
```

```python
import math

import jax
import jax.numpy as jnp
import numpy as np
from jax import lax
from jax.experimental import pallas as pl
from jax.experimental.pallas import tpu as pltpu
from jax.sharding import PartitionSpec as P

LANES = 128
STRIDE = 37
GREETING = 1
POWER = 9
CEILING = 2.0**14
UNROLL = 8
COT_PARTS = 2
SIG_PARTS = 1
LOGICAL = pl.DeviceIdType.LOGICAL
F32 = jnp.float32
BF16 = jnp.bfloat16


def halves(values):
    high = np.asarray(values, np.float32).astype(jnp.bfloat16)
    low = (values - high.astype(np.float64)).astype(jnp.bfloat16)
    return high, low


def tables(seq_count, pieces):
    rows = seq_count * pieces
    length = rows * LANES
    near = np.arange(rows // 2) + 0.5
    odd = np.concatenate([near, rows - near])
    scale = (2.0 / (2 * length)) / math.sqrt(length)
    splits, joins = [], []
    for parity in range(2):
        order = np.concatenate(
            [np.arange(seq_count) * pieces + m for m in range(parity, pieces, 2)]
        )
        angle = 2.0 * math.pi * near[:, None] * order[None, :] / (2 * rows)
        high, low = halves(np.concatenate([np.cos(angle), -np.sin(angle)], axis=0))
        splits.append(np.concatenate([high, low], axis=1))
        joins.append(
            np.stack(halves(np.concatenate([np.cos(angle.T), -np.sin(angle.T)], axis=1) * scale))
        )
    turn = 2.0 * math.pi * odd[:, None] * np.arange(LANES)[None, :] / (2 * length)
    inner = 2.0 * math.pi * np.outer(np.arange(LANES), np.arange(LANES)) / LANES
    cos, sin = np.cos(inner), np.sin(inner)
    ahead = np.block([[cos, -sin], [sin, cos]])
    back = np.block([[cos, sin], [-sin, cos]])
    turns = np.stack([np.cos(turn), -np.sin(turn)]).astype(np.float32)
    return np.stack(splits), np.stack(joins), np.stack(halves(ahead)), np.stack(halves(back)), turns


def parts_of(values):
    high = values.astype(BF16)
    return high, (values - high.astype(F32)).astype(BF16)


def dot(left, right):
    return jnp.dot(left, right, preferred_element_type=F32)


def decode(coded, inverse):
    values = coded.astype(F32)
    size = jnp.abs(values)
    root = jnp.exp2(jnp.log2(size) * (1.0 / POWER)) * inverse
    root = jnp.where(size > 0.0, root, 0.0)
    return jnp.where(values < 0.0, -root, root)


def sweep(start, stop, action, unroll=UNROLL):
    groups = (stop - start) // unroll

    def batch(index, carry):
        for k in range(unroll):
            action(start + index * unroll + k)
        return carry

    lax.fori_loop(0, groups, batch, 0)
    for step in range(start + groups * unroll, stop):
        action(step)


def kernel(seq_count, trace_groups, near_count, cot_h, taps_h, sig_h, split_h, join_h, ahead_h,
           back_h, turns_h, input_out, in_f, scale_out, cot, taps, sig, split, join, ahead, back, turns,
           send_c, send_t, send_s, recv_c, recv_t, recv_s, peak, peaks_near, peak_far, peaks_far,
           sequences, spectra, out_i, out_f, in_i, done_i, scale,
           load_sem, store_sem, send_sem, recv_sem):
    total = seq_count * trace_groups
    held, span, channels = cot.shape
    own = channels // total
    pieces = span // LANES
    traces = held * trace_groups
    rows = seq_count * pieces
    half = rows // 2
    far_count = total // near_count
    seq = lax.axis_index("seq")
    group = lax.axis_index("trace")
    me = seq * trace_groups + group
    cot_parts, sig_parts = send_c.shape[0], send_s.shape[0]
    barrier = pltpu.get_barrier_semaphore()

    loads = [
        pltpu.make_async_copy(src, dst, load_sem.at[n])
        for n, (src, dst) in enumerate(
            [(cot_h, cot), (taps_h, taps), (sig_h, sig), (split_h, split), (join_h, join),
             (ahead_h, ahead), (back_h, back), (turns_h, turns)]
        )
    ]
    for copy in loads:
        copy.start()

    def other(step):
        return lax.rem(me + step * STRIDE, total)

    def crossing(action):
        for turn in range(trace_groups):
            side = lax.rem(group + 1 + turn, trace_groups)
            sweep(
                1 if turn == trace_groups - 1 else 0,
                seq_count,
                lambda step: action(along(step), side),
            )

    def along(step):
        return lax.rem(seq + step * STRIDE, seq_count)

    sweep(1, total, lambda step: pl.semaphore_signal(
        barrier, inc=1, device_id=lax.rem(me + step * GREETING, total), device_id_type=LOGICAL), 32)

    def part(ref, index, parts):
        step = held // parts
        return [ref[i] for i in range(index * step, (index + 1) * step)]

    def spread(blocks):
        turned = [block.T for block in blocks]
        listed = [
            block[c * total : (c + 1) * total, m * LANES : (m + 1) * LANES]
            for block in turned
            for c in range(own)
            for m in range(pieces)
        ]
        return jnp.swapaxes(jnp.stack(listed), 0, 1)

    def largest(values):
        return jnp.max(jnp.abs(values.astype(F32)))

    def push(source, target, slot, device):
        pltpu.make_async_remote_copy(
            src_ref=source,
            dst_ref=target,
            send_sem=send_sem.at[slot],
            recv_sem=recv_sem.at[slot],
            device_id=device,
            device_id_type=LOGICAL,
        ).start()

    def arrive(ref, count, slot):
        view = ref.at[pl.ds(0, count)]
        pltpu.make_async_copy(view, view, recv_sem.at[slot]).wait()

    def depart(ref, count, slot):
        view = ref.at[pl.ds(0, count)]
        pltpu.make_async_copy(view, view, send_sem.at[slot]).wait()

    taps_slot, near_slot, far_slot, filter_slot, input_slot = range(5)
    cot_slot = 5
    sig_slot = 5 + cot_parts

    def send_near(step):
        push(peak, peaks_near.at[second], near_slot,
             first * near_count + lax.rem(second + step, near_count))

    def send_far(step):
        push(peak_far, peaks_far.at[first], far_slot,
             lax.rem(first + step, far_count) * near_count + second)

    def send_taps(step):
        target = along(step) * trace_groups + group
        push(send_t.at[target], recv_t.at[seq], taps_slot, target)

    def send_cot(i):
        return lambda step: push(
            send_c.at[i, other(step)], recv_c.at[i, me], cot_slot + i, other(step))

    def send_sig(i):
        return lambda step: push(
            send_s.at[i, other(step)], recv_s.at[i, me], sig_slot + i, other(step))

    def stage(blocks, send, receive, place):
        send[...] = spread(blocks)
        receive[place] = send[me]

    loads[1].wait()
    stage([taps[...]], send_t, recv_t, seq)
    loads[0].wait()
    stage(part(cot, 0, cot_parts), send_c.at[0], recv_c.at[0], me)
    loads[2].wait()
    lane = lax.broadcasted_iota(jnp.int32, (1, LANES), 1)
    peak[...] = jnp.where(
        lane == 0, largest(cot[...]), jnp.where(lane == 1, largest(taps[...]), largest(sig[...]))
    )
    first = lax.div(me, near_count)
    second = lax.rem(me, near_count)
    peaks_near[second] = peak[...]
    pl.semaphore_wait(barrier, total - 1)
    sweep(1, near_count, send_near)
    sweep(1, seq_count, send_taps)
    sweep(1, total, send_cot(0))
    for i in range(1, cot_parts):
        stage(part(cot, i, cot_parts), send_c.at[i], recv_c.at[i], me)
        sweep(1, total, send_cot(i))
    arrive(peaks_near, near_count - 1, near_slot)
    peak_far[...] = jnp.max(peaks_near[...], axis=0)
    peaks_far[first] = peak_far[...]
    sweep(1, far_count, send_far)
    for i in range(sig_parts):
        stage(part(sig, i, sig_parts), send_s.at[i], recv_s.at[i], me)
        sweep(1, total, send_sig(i))
    for copy in loads[3:]:
        copy.wait()

    def gather(block, items):
        moved = jnp.swapaxes(block, 0, 1)
        for i, item in enumerate(items):
            for parity in range(2):
                columns = [
                    jnp.concatenate(
                        [moved[(i * own + c) * pieces + m] for m in range(parity, pieces, 2)],
                        axis=0,
                    )
                    for c in range(own)
                ]
                sequences[item, parity] = jnp.concatenate(columns, axis=1)

    def gather_groups(blocks, start, stop):
        blocks = blocks.reshape((seq_count, trace_groups) + blocks.shape[1:])
        for side in range(trace_groups):
            gather(blocks[:, side], range(start + side, stop, trace_groups))

    def ahead_first(n):
        sides = []
        for parity in range(2):
            values = sequences[n, parity]
            sides.append(dot(split[parity], jnp.concatenate([values, values], axis=0)))
        even_re, even_im = sides[0][:half], sides[0][half:]
        odd_re, odd_im = sides[1][:half], sides[1][half:]
        real = jnp.concatenate([even_re + odd_re, even_re - odd_re], axis=0)
        imag = jnp.concatenate([even_im + odd_im, odd_im - even_im], axis=0)
        listed = []
        for c in range(own):
            lanes = slice(c * LANES, (c + 1) * LANES)
            re, im = real[:, lanes], imag[:, lanes]
            listed.append(parts_of(jnp.concatenate(
                [re * turns[0] - im * turns[1], re * turns[1] + im * turns[0]], axis=1
            )))
        return listed

    def ahead_second(n, listed):
        for c, (high, low) in enumerate(listed):
            spectra[n, c] = dot(high, ahead[0]) + dot(low, ahead[0]) + dot(high, ahead[1])

    def ahead_all(start, stop):
        waiting = ahead_first(start)
        for n in range(start, stop):
            following = ahead_first(n + 1) if n + 1 < stop else None
            ahead_second(n, waiting)
            waiting = following

    def back_item(products):
        sides = [[], []]
        for product in products:
            high, low = parts_of(product)
            mid = dot(high, back[0]) + dot(low, back[0]) + dot(high, back[1])
            re, im = mid[:, :LANES], mid[:, LANES:]
            real = re * turns[0] + im * turns[1]
            imag = im * turns[0] - re * turns[1]
            sides[0].append(
                jnp.concatenate([real[:half] + real[half:], imag[:half] - imag[half:]], axis=0)
            )
            sides[1].append(
                jnp.concatenate([real[:half] - real[half:], imag[:half] + imag[half:]], axis=0)
            )
        results = []
        for parity in range(2):
            high, low = parts_of(jnp.concatenate(sides[parity], axis=1))
            results.append(
                dot(join[parity, 0], high) + dot(join[parity, 0], low) + dot(join[parity, 1], high)
            )
        return results

    def turned_product(left, right):
        lr, li = left[:, :LANES], left[:, LANES:]
        rr, ri = right[:, :LANES], right[:, LANES:]
        return jnp.concatenate([lr * rr + li * ri, lr * ri - li * rr], axis=1)

    def cut(sides):
        return [
            sides[m % 2][
                (m // 2) * seq_count : (m // 2 + 1) * seq_count, c * LANES : (c + 1) * LANES
            ]
            for c in range(own)
            for m in range(pieces)
        ]

    def encode(values, inverse):
        scaled = values * (1.0 / inverse)
        square = scaled * scaled
        fourth = square * square
        return (fourth * fourth * scaled).astype(BF16)

    first_c, first_s = 1, 1 + traces
    arrive(recv_t, seq_count - 1, taps_slot)
    gather(recv_t[...], [0])
    step = traces // cot_parts
    for i in range(cot_parts):
        arrive(recv_c.at[i], total - 1, cot_slot + i)
        base = first_c + i * step
        gather_groups(recv_c[i], base, base + step)
        ahead_all(base if i else 0, base + step)

    arrive(peaks_far, far_count - 1, far_slot)
    bounds = jnp.max(peaks_far[...], axis=0)

    def bound(position):
        return jnp.max(jnp.where(lane == position, bounds, 0.0), axis=1, keepdims=True)

    reach = math.sqrt(seq_count * span) / CEILING
    inverse_i = jnp.maximum(bound(0) * bound(1) * reach, 2.0**-120)
    inverse_f = jnp.maximum(bound(0) * bound(2) * (reach * traces), 2.0**-120)

    for turn in range(trace_groups):
        side = lax.rem(group + 1 + turn, trace_groups)
        listed = []
        for i in range(held):
            n = first_c + i * trace_groups + side
            sides = back_item([turned_product(spectra[0, c], spectra[n, c]) for c in range(own)])
            listed += cut([encode(values, inverse_i) for values in sides])
        out_i[:, side] = jnp.swapaxes(jnp.stack(listed), 0, 1)

        def send_input(step):
            target = along(step)
            push(out_i.at[target, side], in_i.at[me], input_slot, target * trace_groups + side)

        sweep(1 if turn == trace_groups - 1 else 0, seq_count, send_input)
    in_i[me] = out_i[seq, group]

    sums = [None] * own
    step = traces // sig_parts
    for i in range(sig_parts):
        arrive(recv_s.at[i], total - 1, sig_slot + i)
        base = i * step
        gather_groups(recv_s[i], first_s + base, first_s + base + step)
        ahead_all(first_s + base, first_s + base + step)
        for b in range(base, base + step):
            for c in range(own):
                product = turned_product(spectra[first_s + b, c], spectra[first_c + b, c])
                sums[c] = product if sums[c] is None else sums[c] + product
    coded = cut([encode(values, inverse_f) for values in back_item(sums)])
    out_f[...] = jnp.swapaxes(jnp.stack(coded), 0, 1)
    keep = pltpu.make_async_copy(out_f.at[seq], in_f.at[me], store_sem.at[1])
    keep.start()
    scale[...] = jnp.broadcast_to(inverse_f, scale.shape)
    store_s = pltpu.make_async_copy(scale, scale_out, store_sem.at[2])
    store_s.start()
    crossing(lambda target, side: push(
        out_f.at[target], in_f.at[me], filter_slot, target * trace_groups + side))

    arrive(in_i, total - 1, input_slot)
    moved = jnp.swapaxes(in_i[...], 0, 1)
    for i in range(held):
        for c in range(own):
            for m in range(pieces):
                done_i[i, m * LANES : (m + 1) * LANES, c * total : (c + 1) * total] = decode(
                    moved[(i * own + c) * pieces + m], inverse_i
                ).T
    store_i = pltpu.make_async_copy(done_i, input_out, store_sem.at[0])
    store_i.start()
    arrive(in_f, total - 1, filter_slot)
    depart(recv_t, seq_count - 1, taps_slot)
    for i in range(cot_parts):
        depart(recv_c.at[i], total - 1, cot_slot + i)
    for i in range(sig_parts):
        depart(recv_s.at[i], total - 1, sig_slot + i)
    depart(in_i, total - 1, input_slot)
    depart(in_f, total - 1, filter_slot)
    depart(peaks_near, near_count - 1, near_slot)
    depart(peaks_far, far_count - 1, far_slot)
    store_i.wait()
    keep.wait()
    store_s.wait()


def finish(input_grad, coded, scale, input_out, filter_out, done, store_sem):
    span, channels = filter_out.shape
    total = coded.shape[0]
    pieces = span // LANES
    store_i = pltpu.make_async_copy(input_grad, input_out, store_sem.at[0])
    store_i.start()
    moved = jnp.swapaxes(coded[...], 0, 1)
    stores = [store_i]
    for m in range(pieces):
        rows = pl.ds(m * LANES, LANES)
        for c in range(channels // total):
            done[rows, c * total : (c + 1) * total] = decode(moved[c * pieces + m], scale[...]).T
        stores.append(
            pltpu.make_async_copy(done.at[rows], filter_out.at[rows], store_sem.at[1 + m])
        )
        stores[-1].start()
    for store in stores:
        store.wait()


def local(seq_count, trace_groups, signal, cotangent, filter_taps):
    total = seq_count * trace_groups
    held, span, channels = signal.shape
    own = channels // total
    pieces = span // LANES
    rows = seq_count * pieces
    items = 1 + 2 * held * trace_groups
    near_count = min(16, total // 2)
    constants = [jnp.asarray(table) for table in tables(seq_count, pieces)]
    wide, thin = held * own * pieces, own * pieces
    cot_shape = (COT_PARTS, total, wide // COT_PARTS, LANES)
    sig_shape = (SIG_PARTS, total, wide // SIG_PARTS, LANES)
    inputs = [cotangent, filter_taps, signal, *constants]
    anywhere = pl.BlockSpec(memory_space=pl.ANY)

    def body(*refs):
        kernel(seq_count, trace_groups, near_count, *refs)

    input_grad, coded, scale = pl.pallas_call(
        body,
        out_shape=(
            jax.ShapeDtypeStruct((held, span, channels), F32),
            jax.ShapeDtypeStruct((total, thin, LANES), BF16),
            jax.ShapeDtypeStruct((1, LANES), F32),
        ),
        in_specs=[anywhere] * len(inputs),
        out_specs=(anywhere,) * 3,
        scratch_shapes=[pltpu.VMEM(array.shape, array.dtype) for array in inputs]
        + [
            pltpu.VMEM(cot_shape, BF16),
            pltpu.VMEM((total, thin, LANES), BF16),
            pltpu.VMEM(sig_shape, BF16),
            pltpu.VMEM(cot_shape, BF16),
            pltpu.VMEM((seq_count, thin, LANES), BF16),
            pltpu.VMEM(sig_shape, BF16),
            pltpu.VMEM((1, LANES), F32),
            pltpu.VMEM((near_count, 1, LANES), F32),
            pltpu.VMEM((1, LANES), F32),
            pltpu.VMEM((total // near_count, 1, LANES), F32),
            pltpu.VMEM((items, 2, rows // 2, own * LANES), BF16),
            pltpu.VMEM((items, own, rows, 2 * LANES), F32),
            pltpu.VMEM((seq_count, trace_groups, wide, LANES), BF16),
            pltpu.VMEM((seq_count, thin, LANES), BF16),
            pltpu.VMEM((total, wide, LANES), BF16),
            pltpu.VMEM((held, span, channels), F32),
            pltpu.VMEM((1, LANES), F32),
            pltpu.SemaphoreType.DMA((len(inputs),)),
            pltpu.SemaphoreType.DMA((3,)),
            pltpu.SemaphoreType.DMA((5 + COT_PARTS + SIG_PARTS,)),
            pltpu.SemaphoreType.DMA((5 + COT_PARTS + SIG_PARTS,)),
        ],
        name="correlate",
        compiler_params=pltpu.CompilerParams(
            collective_id=0, has_side_effects=True, vmem_limit_bytes=32 << 20
        ),
    )(*[pltpu.with_memory_space_constraint(x, pltpu.HBM) for x in inputs])
    return pl.pallas_call(
        finish,
        out_shape=(
            jax.ShapeDtypeStruct((held, span, channels), F32),
            jax.ShapeDtypeStruct((span, channels), F32),
        ),
        in_specs=[anywhere, pl.BlockSpec(memory_space=pltpu.VMEM), pl.BlockSpec(memory_space=pltpu.VMEM)],
        out_specs=(anywhere, anywhere),
        scratch_shapes=[pltpu.VMEM((span, channels), F32), pltpu.SemaphoreType.DMA((1 + pieces,))],
        name="finish",
    )(*[pltpu.with_memory_space_constraint(x, pltpu.VMEM) for x in (input_grad, coded, scale)])


def solution(mesh):
    seq_count, trace_groups = mesh.shape["seq"], mesh.shape["trace"]

    def run(signal, cotangent, filter_taps):
        return local(seq_count, trace_groups, signal, cotangent, filter_taps)

    in_specs = (P("trace", "seq", None), P("trace", "seq", None), P("seq", None))
    out_specs = (P("trace", "seq", None), P("seq", None))
    return jax.shard_map(run, mesh=mesh, in_specs=in_specs, out_specs=out_specs, check_vma=False)
```

```python
import math

import jax
import jax.numpy as jnp
import numpy as np
from jax import lax
from jax.experimental import pallas as pl
from jax.experimental.pallas import tpu as pltpu
from jax.sharding import PartitionSpec as P

LANES = 128
STRIDE = 37
GREETING = 1
POWER = 9
CEILING = 2.0**14
UNROLL = 8
COT_PARTS = 2
SIG_PARTS = 1
LOGICAL = pl.DeviceIdType.LOGICAL
F32 = jnp.float32
BF16 = jnp.bfloat16


def halves(values):
    high = np.asarray(values, np.float32).astype(jnp.bfloat16)
    low = (values - high.astype(np.float64)).astype(jnp.bfloat16)
    return high, low


def tables(seq_count, pieces):
    rows = seq_count * pieces
    length = rows * LANES
    near = np.arange(rows // 2) + 0.5
    odd = np.concatenate([near, rows - near])
    scale = (2.0 / (2 * length)) / math.sqrt(length)
    splits, joins = [], []
    for parity in range(2):
        order = np.concatenate(
            [np.arange(seq_count) * pieces + m for m in range(parity, pieces, 2)]
        )
        angle = 2.0 * math.pi * near[:, None] * order[None, :] / (2 * rows)
        high, low = halves(np.concatenate([np.cos(angle), -np.sin(angle)], axis=0))
        splits.append(np.concatenate([high, low], axis=1))
        joins.append(
            np.stack(halves(np.concatenate([np.cos(angle.T), -np.sin(angle.T)], axis=1) * scale))
        )
    turn = 2.0 * math.pi * odd[:, None] * np.arange(LANES)[None, :] / (2 * length)
    inner = 2.0 * math.pi * np.outer(np.arange(LANES), np.arange(LANES)) / LANES
    cos, sin = np.cos(inner), np.sin(inner)
    ahead = np.block([[cos, -sin], [sin, cos]])
    back = np.block([[cos, sin], [-sin, cos]])
    turns = np.stack([np.cos(turn), -np.sin(turn)]).astype(np.float32)
    return np.stack(splits), np.stack(joins), np.stack(halves(ahead)), np.stack(halves(back)), turns


def parts_of(values):
    high = values.astype(BF16)
    return high, (values - high.astype(F32)).astype(BF16)


def dot(left, right):
    return jnp.dot(left, right, preferred_element_type=F32)


def decode(coded, inverse):
    values = coded.astype(F32)
    size = jnp.abs(values)
    root = jnp.exp2(jnp.log2(size) * (1.0 / POWER)) * inverse
    root = jnp.where(size > 0.0, root, 0.0)
    return jnp.where(values < 0.0, -root, root)


def sweep(start, stop, action, unroll=UNROLL):
    groups = (stop - start) // unroll

    def batch(index, carry):
        for k in range(unroll):
            action(start + index * unroll + k)
        return carry

    lax.fori_loop(0, groups, batch, 0)
    for step in range(start + groups * unroll, stop):
        action(step)


def kernel(seq_count, trace_groups, near_count, cot_h, taps_h, sig_h, split_h, join_h, ahead_h,
           back_h, turns_h, input_out, in_f, scale_out, cot, taps, sig, split, join, ahead, back, turns,
           send_c, send_t, send_s, recv_c, recv_t, recv_s, peak, peaks_near, peak_far, peaks_far,
           sequences, spectra, out_i, out_f, in_i, done_i, scale,
           load_sem, store_sem, send_sem, recv_sem):
    total = seq_count * trace_groups
    held, span, channels = cot.shape
    own = channels // total
    pieces = span // LANES
    traces = held * trace_groups
    rows = seq_count * pieces
    half = rows // 2
    far_count = total // near_count
    seq = lax.axis_index("seq")
    group = lax.axis_index("trace")
    me = seq * trace_groups + group
    cot_parts, sig_parts = send_c.shape[0], send_s.shape[0]
    barrier = pltpu.get_barrier_semaphore()

    loads = [
        pltpu.make_async_copy(src, dst, load_sem.at[n])
        for n, (src, dst) in enumerate(
            [(cot_h, cot), (taps_h, taps), (sig_h, sig), (split_h, split), (join_h, join),
             (ahead_h, ahead), (back_h, back), (turns_h, turns)]
        )
    ]
    for copy in loads:
        copy.start()

    def other(step):
        return lax.rem(me + step * STRIDE, total)

    def crossing(action):
        for turn in range(trace_groups):
            side = lax.rem(group + 1 + turn, trace_groups)
            sweep(
                1 if turn == trace_groups - 1 else 0,
                seq_count,
                lambda step: action(along(step), side),
            )

    def along(step):
        return lax.rem(seq + step * STRIDE, seq_count)

    sweep(1, total, lambda step: pl.semaphore_signal(
        barrier, inc=1, device_id=lax.rem(me + step * GREETING, total), device_id_type=LOGICAL), 32)

    def part(ref, index, parts):
        step = held // parts
        return [ref[i] for i in range(index * step, (index + 1) * step)]

    def spread(blocks):
        turned = [block.T for block in blocks]
        listed = [
            block[c * total : (c + 1) * total, m * LANES : (m + 1) * LANES]
            for block in turned
            for c in range(own)
            for m in range(pieces)
        ]
        return jnp.swapaxes(jnp.stack(listed), 0, 1)

    def largest(values):
        return jnp.max(jnp.abs(values.astype(F32)))

    def push(source, target, slot, device):
        pltpu.make_async_remote_copy(
            src_ref=source,
            dst_ref=target,
            send_sem=send_sem.at[slot],
            recv_sem=recv_sem.at[slot],
            device_id=device,
            device_id_type=LOGICAL,
        ).start()

    def arrive(ref, count, slot):
        view = ref.at[pl.ds(0, count)]
        pltpu.make_async_copy(view, view, recv_sem.at[slot]).wait()

    def depart(ref, count, slot):
        view = ref.at[pl.ds(0, count)]
        pltpu.make_async_copy(view, view, send_sem.at[slot]).wait()

    taps_slot, near_slot, far_slot, filter_slot, input_slot = range(5)
    cot_slot = 5
    sig_slot = 5 + cot_parts

    def send_near(step):
        push(peak, peaks_near.at[second], near_slot,
             first * near_count + lax.rem(second + step, near_count))

    def send_far(step):
        push(peak_far, peaks_far.at[first], far_slot,
             lax.rem(first + step, far_count) * near_count + second)

    def send_taps(step):
        target = along(step) * trace_groups + group
        push(send_t.at[target], recv_t.at[seq], taps_slot, target)

    def send_cot(i):
        return lambda step: push(
            send_c.at[i, other(step)], recv_c.at[i, me], cot_slot + i, other(step))

    def send_sig(i):
        return lambda step: push(
            send_s.at[i, other(step)], recv_s.at[i, me], sig_slot + i, other(step))

    def stage(blocks, send, receive, place):
        send[...] = spread(blocks)
        receive[place] = send[me]

    loads[1].wait()
    stage([taps[...]], send_t, recv_t, seq)
    loads[0].wait()
    stage(part(cot, 0, cot_parts), send_c.at[0], recv_c.at[0], me)
    loads[2].wait()
    lane = lax.broadcasted_iota(jnp.int32, (1, LANES), 1)
    peak[...] = jnp.where(
        lane == 0, largest(cot[...]), jnp.where(lane == 1, largest(taps[...]), largest(sig[...]))
    )
    first = lax.div(me, near_count)
    second = lax.rem(me, near_count)
    peaks_near[second] = peak[...]
    pl.semaphore_wait(barrier, total - 1)
    sweep(1, near_count, send_near)
    sweep(1, total, send_cot(0))
    sweep(1, seq_count, send_taps)
    for i in range(1, cot_parts):
        stage(part(cot, i, cot_parts), send_c.at[i], recv_c.at[i], me)
        sweep(1, total, send_cot(i))
    arrive(peaks_near, near_count - 1, near_slot)
    peak_far[...] = jnp.max(peaks_near[...], axis=0)
    peaks_far[first] = peak_far[...]
    sweep(1, far_count, send_far)
    for i in range(sig_parts):
        stage(part(sig, i, sig_parts), send_s.at[i], recv_s.at[i], me)
        sweep(1, total, send_sig(i))
    for copy in loads[3:]:
        copy.wait()

    def gather(block, items):
        moved = jnp.swapaxes(block, 0, 1)
        for i, item in enumerate(items):
            for parity in range(2):
                columns = [
                    jnp.concatenate(
                        [moved[(i * own + c) * pieces + m] for m in range(parity, pieces, 2)],
                        axis=0,
                    )
                    for c in range(own)
                ]
                sequences[item, parity] = jnp.concatenate(columns, axis=1)

    def gather_groups(blocks, start, stop):
        blocks = blocks.reshape((seq_count, trace_groups) + blocks.shape[1:])
        for side in range(trace_groups):
            gather(blocks[:, side], range(start + side, stop, trace_groups))

    def ahead_first(n):
        sides = []
        for parity in range(2):
            values = sequences[n, parity]
            sides.append(dot(split[parity], jnp.concatenate([values, values], axis=0)))
        even_re, even_im = sides[0][:half], sides[0][half:]
        odd_re, odd_im = sides[1][:half], sides[1][half:]
        real = jnp.concatenate([even_re + odd_re, even_re - odd_re], axis=0)
        imag = jnp.concatenate([even_im + odd_im, odd_im - even_im], axis=0)
        listed = []
        for c in range(own):
            lanes = slice(c * LANES, (c + 1) * LANES)
            re, im = real[:, lanes], imag[:, lanes]
            listed.append(parts_of(jnp.concatenate(
                [re * turns[0] - im * turns[1], re * turns[1] + im * turns[0]], axis=1
            )))
        return listed

    def ahead_second(n, listed):
        for c, (high, low) in enumerate(listed):
            spectra[n, c] = dot(high, ahead[0]) + dot(low, ahead[0]) + dot(high, ahead[1])

    def ahead_all(start, stop):
        waiting = ahead_first(start)
        for n in range(start, stop):
            following = ahead_first(n + 1) if n + 1 < stop else None
            ahead_second(n, waiting)
            waiting = following

    def back_item(products):
        sides = [[], []]
        for product in products:
            high, low = parts_of(product)
            mid = dot(high, back[0]) + dot(low, back[0]) + dot(high, back[1])
            re, im = mid[:, :LANES], mid[:, LANES:]
            real = re * turns[0] + im * turns[1]
            imag = im * turns[0] - re * turns[1]
            sides[0].append(
                jnp.concatenate([real[:half] + real[half:], imag[:half] - imag[half:]], axis=0)
            )
            sides[1].append(
                jnp.concatenate([real[:half] - real[half:], imag[:half] + imag[half:]], axis=0)
            )
        results = []
        for parity in range(2):
            high, low = parts_of(jnp.concatenate(sides[parity], axis=1))
            results.append(
                dot(join[parity, 0], high) + dot(join[parity, 0], low) + dot(join[parity, 1], high)
            )
        return results

    def turned_product(left, right):
        lr, li = left[:, :LANES], left[:, LANES:]
        rr, ri = right[:, :LANES], right[:, LANES:]
        return jnp.concatenate([lr * rr + li * ri, lr * ri - li * rr], axis=1)

    def cut(sides):
        return [
            sides[m % 2][
                (m // 2) * seq_count : (m // 2 + 1) * seq_count, c * LANES : (c + 1) * LANES
            ]
            for c in range(own)
            for m in range(pieces)
        ]

    def encode(values, inverse):
        scaled = values * (1.0 / inverse)
        square = scaled * scaled
        fourth = square * square
        return (fourth * fourth * scaled).astype(BF16)

    first_c, first_s = 1, 1 + traces
    arrive(recv_t, seq_count - 1, taps_slot)
    gather(recv_t[...], [0])
    step = traces // cot_parts
    for i in range(cot_parts):
        arrive(recv_c.at[i], total - 1, cot_slot + i)
        base = first_c + i * step
        gather_groups(recv_c[i], base, base + step)
        ahead_all(base if i else 0, base + step)

    arrive(peaks_far, far_count - 1, far_slot)
    bounds = jnp.max(peaks_far[...], axis=0)

    def bound(position):
        return jnp.max(jnp.where(lane == position, bounds, 0.0), axis=1, keepdims=True)

    reach = math.sqrt(seq_count * span) / CEILING
    inverse_i = jnp.maximum(bound(0) * bound(1) * reach, 2.0**-120)
    inverse_f = jnp.maximum(bound(0) * bound(2) * (reach * traces), 2.0**-120)

    for turn in range(trace_groups):
        side = lax.rem(group + 1 + turn, trace_groups)
        listed = []
        for i in range(held):
            n = first_c + i * trace_groups + side
            sides = back_item([turned_product(spectra[0, c], spectra[n, c]) for c in range(own)])
            listed += cut([encode(values, inverse_i) for values in sides])
        out_i[:, side] = jnp.swapaxes(jnp.stack(listed), 0, 1)

        def send_input(step):
            target = along(step)
            push(out_i.at[target, side], in_i.at[me], input_slot, target * trace_groups + side)

        sweep(1 if turn == trace_groups - 1 else 0, seq_count, send_input)
    in_i[me] = out_i[seq, group]

    sums = [None] * own
    step = traces // sig_parts
    for i in range(sig_parts):
        arrive(recv_s.at[i], total - 1, sig_slot + i)
        base = i * step
        gather_groups(recv_s[i], first_s + base, first_s + base + step)
        ahead_all(first_s + base, first_s + base + step)
        for b in range(base, base + step):
            for c in range(own):
                product = turned_product(spectra[first_s + b, c], spectra[first_c + b, c])
                sums[c] = product if sums[c] is None else sums[c] + product
    coded = cut([encode(values, inverse_f) for values in back_item(sums)])
    out_f[...] = jnp.swapaxes(jnp.stack(coded), 0, 1)
    keep = pltpu.make_async_copy(out_f.at[seq], in_f.at[me], store_sem.at[1])
    keep.start()
    scale[...] = jnp.broadcast_to(inverse_f, scale.shape)
    store_s = pltpu.make_async_copy(scale, scale_out, store_sem.at[2])
    store_s.start()
    crossing(lambda target, side: push(
        out_f.at[target], in_f.at[me], filter_slot, target * trace_groups + side))

    arrive(in_i, total - 1, input_slot)
    moved = jnp.swapaxes(in_i[...], 0, 1)
    for i in range(held):
        for c in range(own):
            for m in range(pieces):
                done_i[i, m * LANES : (m + 1) * LANES, c * total : (c + 1) * total] = decode(
                    moved[(i * own + c) * pieces + m], inverse_i
                ).T
    store_i = pltpu.make_async_copy(done_i, input_out, store_sem.at[0])
    store_i.start()
    arrive(in_f, total - 1, filter_slot)
    depart(recv_t, seq_count - 1, taps_slot)
    for i in range(cot_parts):
        depart(recv_c.at[i], total - 1, cot_slot + i)
    for i in range(sig_parts):
        depart(recv_s.at[i], total - 1, sig_slot + i)
    depart(in_i, total - 1, input_slot)
    depart(in_f, total - 1, filter_slot)
    depart(peaks_near, near_count - 1, near_slot)
    depart(peaks_far, far_count - 1, far_slot)
    store_i.wait()
    keep.wait()
    store_s.wait()


def finish(input_grad, coded, scale, input_out, filter_out, done, store_sem):
    span, channels = filter_out.shape
    total = coded.shape[0]
    pieces = span // LANES
    store_i = pltpu.make_async_copy(input_grad, input_out, store_sem.at[0])
    store_i.start()
    moved = jnp.swapaxes(coded[...], 0, 1)
    stores = [store_i]
    for m in range(pieces):
        rows = pl.ds(m * LANES, LANES)
        for c in range(channels // total):
            done[rows, c * total : (c + 1) * total] = decode(moved[c * pieces + m], scale[...]).T
        stores.append(
            pltpu.make_async_copy(done.at[rows], filter_out.at[rows], store_sem.at[1 + m])
        )
        stores[-1].start()
    for store in stores:
        store.wait()


def local(seq_count, trace_groups, signal, cotangent, filter_taps):
    total = seq_count * trace_groups
    held, span, channels = signal.shape
    own = channels // total
    pieces = span // LANES
    rows = seq_count * pieces
    items = 1 + 2 * held * trace_groups
    near_count = min(16, total // 2)
    constants = [jnp.asarray(table) for table in tables(seq_count, pieces)]
    wide, thin = held * own * pieces, own * pieces
    cot_shape = (COT_PARTS, total, wide // COT_PARTS, LANES)
    sig_shape = (SIG_PARTS, total, wide // SIG_PARTS, LANES)
    inputs = [cotangent, filter_taps, signal, *constants]
    anywhere = pl.BlockSpec(memory_space=pl.ANY)

    def body(*refs):
        kernel(seq_count, trace_groups, near_count, *refs)

    input_grad, coded, scale = pl.pallas_call(
        body,
        out_shape=(
            jax.ShapeDtypeStruct((held, span, channels), F32),
            jax.ShapeDtypeStruct((total, thin, LANES), BF16),
            jax.ShapeDtypeStruct((1, LANES), F32),
        ),
        in_specs=[anywhere] * len(inputs),
        out_specs=(anywhere,) * 3,
        scratch_shapes=[pltpu.VMEM(array.shape, array.dtype) for array in inputs]
        + [
            pltpu.VMEM(cot_shape, BF16),
            pltpu.VMEM((total, thin, LANES), BF16),
            pltpu.VMEM(sig_shape, BF16),
            pltpu.VMEM(cot_shape, BF16),
            pltpu.VMEM((seq_count, thin, LANES), BF16),
            pltpu.VMEM(sig_shape, BF16),
            pltpu.VMEM((1, LANES), F32),
            pltpu.VMEM((near_count, 1, LANES), F32),
            pltpu.VMEM((1, LANES), F32),
            pltpu.VMEM((total // near_count, 1, LANES), F32),
            pltpu.VMEM((items, 2, rows // 2, own * LANES), BF16),
            pltpu.VMEM((items, own, rows, 2 * LANES), F32),
            pltpu.VMEM((seq_count, trace_groups, wide, LANES), BF16),
            pltpu.VMEM((seq_count, thin, LANES), BF16),
            pltpu.VMEM((total, wide, LANES), BF16),
            pltpu.VMEM((held, span, channels), F32),
            pltpu.VMEM((1, LANES), F32),
            pltpu.SemaphoreType.DMA((len(inputs),)),
            pltpu.SemaphoreType.DMA((3,)),
            pltpu.SemaphoreType.DMA((5 + COT_PARTS + SIG_PARTS,)),
            pltpu.SemaphoreType.DMA((5 + COT_PARTS + SIG_PARTS,)),
        ],
        name="correlate",
        compiler_params=pltpu.CompilerParams(
            collective_id=0, has_side_effects=True, vmem_limit_bytes=32 << 20
        ),
    )(*[pltpu.with_memory_space_constraint(x, pltpu.HBM) for x in inputs])
    return pl.pallas_call(
        finish,
        out_shape=(
            jax.ShapeDtypeStruct((held, span, channels), F32),
            jax.ShapeDtypeStruct((span, channels), F32),
        ),
        in_specs=[anywhere, pl.BlockSpec(memory_space=pltpu.VMEM), pl.BlockSpec(memory_space=pltpu.VMEM)],
        out_specs=(anywhere, anywhere),
        scratch_shapes=[pltpu.VMEM((span, channels), F32), pltpu.SemaphoreType.DMA((1 + pieces,))],
        name="finish",
    )(*[pltpu.with_memory_space_constraint(x, pltpu.VMEM) for x in (input_grad, coded, scale)])


def solution(mesh):
    seq_count, trace_groups = mesh.shape["seq"], mesh.shape["trace"]

    def run(signal, cotangent, filter_taps):
        return local(seq_count, trace_groups, signal, cotangent, filter_taps)

    in_specs = (P("trace", "seq", None), P("trace", "seq", None), P("seq", None))
    out_specs = (P("trace", "seq", None), P("seq", None))
    return jax.shard_map(run, mesh=mesh, in_specs=in_specs, out_specs=out_specs, check_vma=False)
```
